128 devices in a mesh: dp: 16 (over x, z_lo, core), ctx: 8 (over z_hi, y).
Axes of the slice: x: 4, y: 4, z: 4 (z_hi: 2, z_lo: 2; z = z_hi * 2 + z_lo), core: 2. Of those that a mesh axis runs over, the one named last changes fastest.
Arguments:
- document: bfloat16 [16, 2048, 1024], P('dp', 'ctx'), may hold values from -45 to 45, as said below
- summary: bfloat16 [16, 1024, 1024], P('dp', 'ctx'), may hold values from -45 to 45, as said below
- encoder_gain: float32 [1024], replicated, may hold values from 0.5 to 1.5
- query_weight: bfloat16 [1024, 1024], replicated, as said below
- key_weight: bfloat16 [1024, 1024], replicated, as said below
- value_weight: bfloat16 [1024, 1024], replicated, may hold values from -0.1875 to 0.1875
- output_weight: bfloat16 [1024, 1024], replicated, may hold values from -0.1875 to 0.1875
- memory_gain: float32 [1024], replicated, may hold values from 0.5 to 1.5
- summary_gain: float32 [1024], replicated, may hold values from 0.5 to 1.5
- cross_query: bfloat16 [1024, 1024], replicated, as said below
- cross_key: bfloat16 [1024, 1024], replicated, as said below
- cross_value: bfloat16 [1024, 1024], replicated, may hold values from -0.1875 to 0.1875
- cross_output: bfloat16 [1024, 1024], replicated, may hold values from -0.1875 to 0.1875
- encoder_cotangent: bfloat16 [16, 2048, 1024], P('dp', 'ctx'), as said below
- decoder_cotangent: bfloat16 [16, 1024, 1024], P('dp', 'ctx'), as said below
Outputs:
- encoded: bfloat16 [16, 2048, 1024], P('dp', 'ctx')
- decoded: bfloat16 [16, 1024, 1024], P('dp', 'ctx')
- output_grad: bfloat16 [1024, 1024], replicated
- cross_grad: bfloat16 [1024, 1024], replicated
The draws below stay inside these ranges and needn't reach their ends.
Inputs may be any that keep to these rules, and one draw needn't show every extreme that they name: `document`: encoder states of order one. `summary`: decoder states of order one. `query_weight`: entries of order one over the square root of 1024. `key_weight`: entries of order one over the square root of 1024. `cross_query`: entries of order one over the square root of 1024. `cross_key`: entries of order one over the square root of 1024. `encoder_cotangent`: entries of order one over the square root of 32768. `decoder_cotangent`: entries of order one over the square root of 16384.
All inputs are finite; a program needn't handle non-finite values.
Results may differ from the reference program's by a relative error of at most 0.035.
The reference program's roundings to bfloat16 on the way (of `normed`, `heads`, `summary_query` and `cross_heads`) count: a program that leaves them out, or rounds other values in their place, can miss the bound.
Values may be sent and summed in bfloat16 or wider, within the bound.
A program may use at most 192 MiB of HBM per device.

```python
import jax
import jax.numpy as jnp
from jax import lax

D = 1024
HEADS = 16
HEAD_DIM = 64
GROUPS = 16
DOC_LEN = 2048
SUM_LEN = 1024


def document_rows(key):
    base_key = jax.random.fold_in(key, 1)
    return jnp.clip(jax.random.normal(base_key, (GROUPS, DOC_LEN, D), jnp.float32), -4.0, 4.0)


def draw_document(key, part):
    return document_rows(key).astype(jnp.bfloat16)


def draw_summary(key, part):
    rows = jnp.clip(jax.random.normal(jax.random.fold_in(key, 6), (GROUPS, SUM_LEN, D), jnp.float32), -4.0, 4.0)
    return rows.astype(jnp.bfloat16)


def paired_weight(key, salt, which):
    spread = D ** (-0.5)
    own = jnp.clip(jax.random.normal(jax.random.fold_in(key, salt + which + 30), (D, D), jnp.float32), -4.0, 4.0)
    return own * spread


def draw_query_weight(key, part):
    return paired_weight(key, 40, 1).astype(jnp.bfloat16)


def draw_key_weight(key, part):
    return paired_weight(key, 40, 2).astype(jnp.bfloat16)


def draw_cross_query(key, part):
    return paired_weight(key, 60, 1).astype(jnp.bfloat16)


def draw_cross_key(key, part):
    return paired_weight(key, 60, 2).astype(jnp.bfloat16)


def cotangent_rows(key, salt, count):
    scale = (GROUPS * count) ** (-0.5)
    return jnp.clip(jax.random.normal(jax.random.fold_in(key, salt + 2), (GROUPS, count, D), jnp.float32), -4.0, 4.0) * scale


def draw_encoder_cotangent(key, part):
    return cotangent_rows(key, 80, DOC_LEN).astype(jnp.bfloat16)


def draw_decoder_cotangent(key, part):
    return cotangent_rows(key, 90, SUM_LEN).astype(jnp.bfloat16)


def scatter_about(rng, dims, scale, limit, kind=jnp.bfloat16):
    entries = jax.random.normal(rng, dims, jnp.float32) * scale
    return jnp.minimum(jnp.maximum(entries, -limit), limit).astype(kind)


def setup_inputs(seed: int = 0) -> dict:
    key_of = jax.random.split(jax.random.key(seed), 16)
    return {
        "document": draw_document(jax.random.fold_in(key_of[15], 71), 0),
        "summary": draw_summary(jax.random.fold_in(key_of[15], 71), 0),
        "encoder_gain": jnp.clip(1.0 + 0.1 * jax.random.normal(key_of[2], (D,), jnp.float32), 0.5, 1.5),
        "query_weight": draw_query_weight(jax.random.fold_in(key_of[15], 71), 0),
        "key_weight": draw_key_weight(jax.random.fold_in(key_of[15], 71), 0),
        "value_weight": scatter_about(key_of[5], (D, D), D ** -0.5, 0.1875),
        "output_weight": scatter_about(key_of[6], (D, D), D ** -0.5, 0.1875),
        "memory_gain": jnp.clip(1.0 + 0.1 * jax.random.normal(key_of[7], (D,), jnp.float32), 0.5, 1.5),
        "summary_gain": jnp.clip(1.0 + 0.1 * jax.random.normal(key_of[8], (D,), jnp.float32), 0.5, 1.5),
        "cross_query": draw_cross_query(jax.random.fold_in(key_of[15], 71), 0),
        "cross_key": draw_cross_key(jax.random.fold_in(key_of[15], 71), 0),
        "cross_value": scatter_about(key_of[11], (D, D), D ** -0.5, 0.1875),
        "cross_output": scatter_about(key_of[12], (D, D), D ** -0.5, 0.1875),
        "encoder_cotangent": draw_encoder_cotangent(jax.random.fold_in(key_of[15], 71), 0),
        "decoder_cotangent": draw_decoder_cotangent(jax.random.fold_in(key_of[15], 71), 0),
    }


def norm_rows(rows, gain):
    values = rows.astype(jnp.float32)
    scale = lax.rsqrt(lax.optimization_barrier(jnp.mean(values * values, axis=-1, keepdims=True)) + 1e-06)
    return (values * scale * gain).astype(jnp.bfloat16)

def pick_block(count):
    block = min(512, count)
    while count % block != 0:
        block = block - 1
    return block

def attend(query, keys, values):
    count = query.shape[0]
    block = pick_block(count)
    k_heads = keys.astype(jnp.float32).reshape(keys.shape[0], HEADS, HEAD_DIM)
    v_heads = values.astype(jnp.float32).reshape(values.shape[0], HEADS, HEAD_DIM)

    def one_block(part_rows):
        q_heads = part_rows.astype(jnp.float32).reshape(block, HEADS, HEAD_DIM)
        scores = jnp.einsum('qhd,khd->hqk', q_heads, k_heads, precision=lax.Precision.HIGHEST)
        top = lax.optimization_barrier(jnp.max(scores, axis=-1, keepdims=True))
        weights = jnp.exp(scores - top)
        total = lax.optimization_barrier(jnp.sum(weights, axis=-1))
        rounded = lax.optimization_barrier(weights.astype(jnp.bfloat16)).astype(jnp.float32)
        mixed = jnp.einsum('hqk,khd->qhd', rounded, v_heads, precision=lax.Precision.HIGHEST)
        mixed = mixed / jnp.transpose(total)[:, :, None]
        return mixed.reshape(block, HEADS * HEAD_DIM).astype(jnp.bfloat16)
    blocks = lax.map(one_block, query.reshape(count // block, block, query.shape[1]))
    return blocks.reshape(count, HEADS * HEAD_DIM)

def reference(document, summary, encoder_gain, query_weight, key_weight, value_weight, output_weight, memory_gain, summary_gain, cross_query, cross_key, cross_value, cross_output, encoder_cotangent, decoder_cotangent):

    def one_group(pair):
        rows, states = pair
        normed = norm_rows(rows, encoder_gain)
        query = jnp.dot(normed, query_weight, preferred_element_type=jnp.float32).astype(jnp.bfloat16)
        keys = jnp.dot(normed, key_weight, preferred_element_type=jnp.float32).astype(jnp.bfloat16)
        values = jnp.dot(normed, value_weight, preferred_element_type=jnp.float32).astype(jnp.bfloat16)
        heads = attend(query, keys, values)
        encoded = (rows.astype(jnp.float32) + jnp.dot(heads, output_weight, preferred_element_type=jnp.float32)).astype(jnp.bfloat16)
        memory = norm_rows(encoded, memory_gain)
        memory_keys = jnp.dot(memory, cross_key, preferred_element_type=jnp.float32).astype(jnp.bfloat16)
        memory_values = jnp.dot(memory, cross_value, preferred_element_type=jnp.float32).astype(jnp.bfloat16)
        summary_query = jnp.dot(norm_rows(states, summary_gain), cross_query, preferred_element_type=jnp.float32).astype(jnp.bfloat16)
        cross_heads = attend(summary_query, memory_keys, memory_values)
        decoded = (states.astype(jnp.float32) + jnp.dot(cross_heads, cross_output, preferred_element_type=jnp.float32)).astype(jnp.bfloat16)
        return (heads, encoded, cross_heads, decoded)
    heads, encoded, cross_heads, decoded = lax.map(one_group, (document, summary))
    output_grad = jnp.einsum('gtd,gte->de', heads.astype(jnp.float32), encoder_cotangent.astype(jnp.float32), precision=lax.Precision.HIGHEST)
    cross_grad = jnp.einsum('gtd,gte->de', cross_heads.astype(jnp.float32), decoder_cotangent.astype(jnp.float32), precision=lax.Precision.HIGHEST)
    return (encoded, decoded, output_grad.astype(jnp.bfloat16), cross_grad.astype(jnp.bfloat16))
```

```python
import functools

import jax
import jax.numpy as jnp
from jax import lax
from jax.experimental import pallas as pl
from jax.experimental.pallas import tpu as pltpu
from jax.sharding import PartitionSpec as P

HEADS = 16
HEAD_DIM = 64
LANES = 128
MESH = pl.DeviceIdType.MESH
QKV, SQ, HEAD, KV, CROSS = range(5)


def norm_rows(rows, gain):
    values = rows.astype(jnp.float32)
    scale = lax.rsqrt(jnp.mean(values * values, axis=-1, keepdims=True) + 1e-06)
    return (values * scale * gain).astype(jnp.bfloat16)


def matmul(left, right):
    return jnp.dot(left, right, preferred_element_type=jnp.float32)


def layer_kernel(
    n,
    document,
    summary,
    encoder_gain,
    memory_gain,
    summary_gain,
    query_weight,
    key_weight,
    value_weight,
    output_weight,
    cross_query,
    cross_key,
    cross_value,
    cross_output,
    encoded_out,
    decoded_out,
    heads_out,
    cross_out,
    doc,
    states,
    weights,
    normed,
    qkv_send,
    qkv_recv,
    sq_send,
    sq_recv,
    head_send,
    head_recv,
    kv_send,
    kv_recv,
    cross_send,
    cross_recv,
    value_low,
    value_high,
    encoded,
    decoded,
    load_sem,
    store_sem,
    send_sem,
    recv_sem,
):
    dp = lax.axis_index("dp")
    me = lax.axis_index("ctx")
    rows = doc.shape[0]
    count = states.shape[0]
    width = doc.shape[1]
    blocks = width // (2 * LANES)

    loads = [
        pltpu.make_async_copy(src, dst, load_sem.at[i])
        for i, (src, dst) in enumerate(
            [
                (document, doc),
                (query_weight, weights.at[0]),
                (key_weight, weights.at[1]),
                (value_weight, weights.at[2]),
                (summary, states),
                (cross_query, weights.at[4]),
                (output_weight, weights.at[3]),
                (cross_key, weights.at[5]),
                (cross_value, weights.at[6]),
                (cross_output, weights.at[7]),
            ]
        )
    ]
    for load in loads:
        load.start()

    barrier = pltpu.get_barrier_semaphore()

    @pl.loop(1, n)
    def _(i):
        peer = lax.rem(me + i, n)
        pl.semaphore_signal(barrier, inc=1, device_id=(dp, peer), device_id_type=MESH)

    def remote(phase, peer, source, src, dst):
        return pltpu.make_async_remote_copy(
            src_ref=src,
            dst_ref=dst,
            send_sem=send_sem.at[phase, peer],
            recv_sem=recv_sem.at[phase, source],
            device_id=(dp, peer),
            device_id_type=MESH,
        )

    def local(phase, src, dst):
        return pltpu.make_async_copy(src, dst, recv_sem.at[phase, me])

    def start(phase, peer, src, dst):
        @pl.when(peer != me)
        def _():
            remote(phase, peer, me, src, dst).start()

        @pl.when(peer == me)
        def _():
            local(phase, src, dst).start()

    def wait_all(phase, src_of, dst_of):
        @pl.loop(0, n)
        def _(source):
            @pl.when(source != me)
            def _():
                remote(phase, source, source, src_of(source), dst_of(source)).wait_recv()

            @pl.when(source == me)
            def _():
                local(phase, src_of(source), dst_of(source)).wait()

    def wait_sent(phase, src_of, dst_of):
        @pl.loop(0, n)
        def _(peer):
            @pl.when(peer != me)
            def _():
                remote(phase, peer, me, src_of(peer), dst_of(peer)).wait_send()

    def column(index):
        return pl.ds(pl.multiple_of(index * LANES, LANES), LANES)

    def wide(index):
        return pl.ds(pl.multiple_of(index * 2 * LANES, 2 * LANES), 2 * LANES)

    loads[0].wait()
    normed[...] = norm_rows(doc[...], encoder_gain[...])
    for i in (1, 2, 3):
        loads[i].wait()
    pl.semaphore_wait(barrier, n - 1)

    @pl.loop(0, blocks)
    def _(i):
        block = lax.rem(lax.div(me, 2) + (blocks - 1) - i, blocks)
        for t in range(3):
            part = matmul(normed[...], weights[t, :, wide(block)]).astype(jnp.bfloat16)
            qkv_send[2 * block, t] = part[:, :LANES]
            qkv_send[2 * block + 1, t] = part[:, LANES:]
        for half in range(2):
            peer = 2 * block + half
            start(QKV, peer, qkv_send.at[peer], qkv_recv.at[:, me])

    loads[4].wait()
    loads[5].wait()
    normed[0:count, :] = norm_rows(states[...], summary_gain[...])

    @pl.loop(0, blocks)
    def _(i):
        block = lax.rem(lax.div(me, 2) + (blocks - 1) - i, blocks)
        part = matmul(normed[0:count, :], weights[4, :, wide(block)]).astype(jnp.bfloat16)
        sq_send[2 * block] = part[:, :LANES]
        sq_send[2 * block + 1] = part[:, LANES:]
        for half in range(2):
            peer = 2 * block + half
            start(SQ, peer, sq_send.at[peer], sq_recv.at[me])

    lane = lax.broadcasted_iota(jnp.int32, (1, LANES), 1)
    low = lane < HEAD_DIM
    zero = jnp.zeros((), jnp.bfloat16)
    one = jnp.ones((), jnp.bfloat16)

    def set_values(ref):
        values = ref[...].reshape(n * rows, LANES)
        value_low[...] = jnp.where(low, values, one)
        value_high[...] = jnp.where(low, one, values)

    def attend(query, keys):
        def head(part, values):
            scores = lax.dot_general(
                part, keys, (((1,), (1,)), ((), ())), preferred_element_type=jnp.float32
            )
            top = jnp.max(scores, axis=-1, keepdims=True)
            weight = jnp.exp(scores - top).astype(jnp.bfloat16)
            return matmul(weight, values[...])

        left = head(jnp.where(low, query, zero), value_low)
        right = head(jnp.where(low, zero, query), value_high)
        mixed = jnp.where(low, left, right)
        total = jnp.where(
            low, pltpu.roll(left, HEAD_DIM, 1), pltpu.roll(right, HEAD_DIM, 1)
        )
        return (mixed / total).astype(jnp.bfloat16)

    wait_all(QKV, lambda s: qkv_send.at[s], lambda s: qkv_recv.at[:, s])
    set_values(qkv_recv.at[2])

    @pl.loop(0, n)
    def _(i):
        peer = lax.rem(me + 1 + i, n)
        keys = qkv_recv[1].reshape(n * rows, LANES)
        head_send[peer] = attend(qkv_recv[0, peer], keys)
        start(HEAD, peer, head_send.at[peer], head_recv.at[:, column(me)])

    loads[6].wait()
    wait_all(HEAD, lambda s: head_send.at[s], lambda s: head_recv.at[:, column(s)])

    @pl.loop(0, blocks)
    def _(i):
        mixed = matmul(head_recv[...], weights[3, :, wide(i)])
        encoded[:, wide(i)] = (doc[:, wide(i)].astype(jnp.float32) + mixed).astype(jnp.bfloat16)

    stores = [
        pltpu.make_async_copy(src, dst, store_sem.at[i])
        for i, (src, dst) in enumerate(
            [
                (encoded, encoded_out),
                (head_recv, heads_out),
                (decoded, decoded_out),
                (cross_recv, cross_out),
            ]
        )
    ]
    stores[0].start()
    stores[1].start()

    normed[...] = norm_rows(encoded[...], memory_gain[...])
    loads[7].wait()
    loads[8].wait()

    @pl.loop(0, blocks)
    def _(i):
        block = lax.rem(lax.div(me, 2) + (blocks - 1) - i, blocks)
        for t in range(2):
            part = matmul(normed[...], weights[5 + t, :, wide(block)]).astype(jnp.bfloat16)
            kv_send[2 * block, t] = part[:, :LANES]
            kv_send[2 * block + 1, t] = part[:, LANES:]
        for half in range(2):
            peer = 2 * block + half
            start(KV, peer, kv_send.at[peer], kv_recv.at[:, me])

    wait_all(SQ, lambda s: sq_send.at[s], lambda s: sq_recv.at[s])
    wait_all(KV, lambda s: kv_send.at[s], lambda s: kv_recv.at[:, s])
    set_values(kv_recv.at[1])

    @pl.loop(0, n // 2)
    def _(i):
        pair = lax.rem(lax.div(me, 2) + 1 + i, n // 2)
        keys = kv_recv[0].reshape(n * rows, LANES)
        query = sq_recv[pl.ds(2 * pair, 2)].reshape(2 * count, LANES)
        mixed = attend(query, keys)
        cross_send[2 * pair] = mixed[:count]
        cross_send[2 * pair + 1] = mixed[count:]
        for half in range(2):
            peer = 2 * pair + half
            start(CROSS, peer, cross_send.at[peer], cross_recv.at[:, column(me)])

    loads[9].wait()
    wait_all(CROSS, lambda s: cross_send.at[s], lambda s: cross_recv.at[:, column(s)])

    @pl.loop(0, blocks)
    def _(i):
        mixed = matmul(cross_recv[...], weights[7, :, wide(i)])
        decoded[:, wide(i)] = (states[:, wide(i)].astype(jnp.float32) + mixed).astype(jnp.bfloat16)

    stores[2].start()
    stores[3].start()
    wait_sent(QKV, lambda p: qkv_send.at[p], lambda p: qkv_recv.at[:, me])
    wait_sent(SQ, lambda p: sq_send.at[p], lambda p: sq_recv.at[me])
    wait_sent(HEAD, lambda p: head_send.at[p], lambda p: head_recv.at[:, column(me)])
    wait_sent(KV, lambda p: kv_send.at[p], lambda p: kv_recv.at[:, me])
    wait_sent(CROSS, lambda p: cross_send.at[p], lambda p: cross_recv.at[:, column(me)])
    for store in stores:
        store.wait()


def row_products(left, right):
    return lax.dot_general(
        left, right, (((0,), (0,)), ((), ())), preferred_element_type=jnp.float32
    )


def solution(mesh):
    n = mesh.shape["ctx"]

    def body(
        document,
        summary,
        encoder_gain,
        query_weight,
        key_weight,
        value_weight,
        output_weight,
        memory_gain,
        summary_gain,
        cross_query,
        cross_key,
        cross_value,
        cross_output,
        encoder_cotangent,
        decoder_cotangent,
    ):
        rows, width = document.shape[1:]
        count = summary.shape[1]
        half = jnp.bfloat16
        hbm = pl.BlockSpec(memory_space=pl.ANY)
        vmem = pl.BlockSpec(memory_space=pltpu.VMEM)
        encoded, decoded, heads, cross_heads = pl.pallas_call(
            functools.partial(layer_kernel, n),
            out_shape=[
                jax.ShapeDtypeStruct((rows, width), half),
                jax.ShapeDtypeStruct((count, width), half),
                jax.ShapeDtypeStruct((rows, width), half),
                jax.ShapeDtypeStruct((count, width), half),
            ],
            in_specs=[hbm] * 2 + [vmem] * 3 + [hbm] * 8,
            out_specs=[hbm] * 4,
            scratch_shapes=[
                pltpu.VMEM((rows, width), half),
                pltpu.VMEM((count, width), half),
                pltpu.VMEM((8, width, width), half),
                pltpu.VMEM((rows, width), half),
                pltpu.VMEM((n, 3, rows, LANES), half),
                pltpu.VMEM((3, n, rows, LANES), half),
                pltpu.VMEM((n, count, LANES), half),
                pltpu.VMEM((n, count, LANES), half),
                pltpu.VMEM((n, rows, LANES), half),
                pltpu.VMEM((rows, width), half),
                pltpu.VMEM((n, 2, rows, LANES), half),
                pltpu.VMEM((2, n, rows, LANES), half),
                pltpu.VMEM((n, count, LANES), half),
                pltpu.VMEM((count, width), half),
                pltpu.VMEM((n * rows, LANES), half),
                pltpu.VMEM((n * rows, LANES), half),
                pltpu.VMEM((rows, width), half),
                pltpu.VMEM((count, width), half),
                pltpu.SemaphoreType.DMA((10,)),
                pltpu.SemaphoreType.DMA((4,)),
                pltpu.SemaphoreType.DMA((5, n)),
                pltpu.SemaphoreType.DMA((5, n)),
            ],
            compiler_params=pltpu.CompilerParams(
                collective_id=0, has_side_effects=True, vmem_limit_bytes=56 * 2**20
            ),
        )(
            document[0],
            summary[0],
            encoder_gain[None],
            memory_gain[None],
            summary_gain[None],
            query_weight,
            key_weight,
            value_weight,
            output_weight,
            cross_query,
            cross_key,
            cross_value,
            cross_output,
        )
        own_local = row_products(heads, encoder_cotangent[0])
        cross_local = row_products(cross_heads, decoder_cotangent[0])
        own_sum, cross_sum = lax.psum((own_local, cross_local), ("dp", "ctx"))
        return (
            encoded[None],
            decoded[None],
            own_sum.astype(jnp.bfloat16),
            cross_sum.astype(jnp.bfloat16),
        )

    rows_spec = P("dp", "ctx", None)
    return jax.shard_map(
        body,
        mesh=mesh,
        in_specs=(rows_spec, rows_spec) + (P(),) * 11 + (rows_spec, rows_spec),
        out_specs=(rows_spec, rows_spec, P(), P()),
        check_vma=False,
    )
```

```python
import functools

import jax
import jax.numpy as jnp
from jax import lax
from jax.experimental import pallas as pl
from jax.experimental.pallas import tpu as pltpu
from jax.sharding import PartitionSpec as P

HEADS = 16
HEAD_DIM = 64
LANES = 128
MESH = pl.DeviceIdType.MESH
QKV, SQ, HEAD, KV, CROSS = range(5)


def norm_rows(rows, gain):
    values = rows.astype(jnp.float32)
    scale = lax.rsqrt(jnp.mean(values * values, axis=-1, keepdims=True) + 1e-06)
    return (values * scale * gain).astype(jnp.bfloat16)


def matmul(left, right):
    return jnp.dot(left, right, preferred_element_type=jnp.float32)


OWN_PARTS = ((0, 1024, "xyz"),)
CROSS_PARTS = ((0, 512, "xyz"), (512, 256, "yzx"), (768, 256, "zxy"))
REFS = 11


class Neighbours:
    def __init__(self, dp, ctx):
        self.core = lax.rem(dp, 2)
        self.x = lax.div(dp, 4)
        self.y = lax.rem(ctx, 4)
        self.z = lax.div(ctx, 4) * 2 + lax.rem(lax.div(dp, 2), 2)
        self.sibling = self.device(self.x, self.y, self.z, 1 - self.core)

    def device(self, x, y, z, core):
        return (x * 4 + lax.rem(z, 2) * 2 + core, lax.div(z, 2) * 4 + y)

    def place(self, axis):
        return {"x": self.x, "y": self.y, "z": self.z}[axis]

    def at(self, axis, step):
        place = {"x": self.x, "y": self.y, "z": self.z}
        place[axis] = lax.rem(place[axis] + step, 4)
        return self.device(place["x"], place["y"], place["z"], self.core)


def aligned(start, size):
    return pl.ds(pl.multiple_of(start, size), size)


class Reduction:
    def __init__(
        self, near, parts, partial, pair, first, first_in, second, second_in, third, third_in, full, send, recv
    ):
        self.near = near
        self.parts = parts
        self.partial, self.pair, self.full = partial, pair, full
        self.held = [first, second, third]
        self.incoming = [first_in, second_in, third_in]
        self.send, self.recv = send, recv
        self.half = pair.shape[0]
        self.base = near.core * self.half
        self.started = []

    def copy(self, src, dst, slot, device):
        return pltpu.make_async_remote_copy(
            src_ref=src,
            dst_ref=dst,
            send_sem=self.send.at[slot],
            recv_sem=self.recv.at[slot],
            device_id=device,
            device_id_type=MESH,
        )

    def product(self, left, right):
        step = 256

        @pl.loop(0, left.shape[1] // step)
        def _(i):
            block = lax.rem(i + (1 - self.near.core) * (self.half // step), left.shape[1] // step)
            rows = aligned(block * step, step)
            mixed = lax.dot_general(
                left[:, rows], right[...], (((0,), (0,)), ((), ())), preferred_element_type=jnp.float32
            )
            self.partial[rows, :] = mixed.astype(jnp.bfloat16)

        other = (1 - self.near.core) * self.half
        self.pair_copy = self.copy(
            self.partial.at[aligned(other, self.half)], self.pair, 0, self.near.sibling
        )
        self.pair_copy.start()
        self.started.append(self.pair_copy)

    def pair_sum(self):
        self.pair_copy.wait_recv()
        step = 128

        @pl.loop(0, self.half // step)
        def _(i):
            own = self.partial[aligned(self.base + i * step, step), :].astype(jnp.float32)
            rows = aligned(i * step, step)
            total = own + self.pair[rows, :].astype(jnp.float32)
            self.held[0][rows, :] = total.astype(jnp.bfloat16)

        self.copies = {}
        self.start_scatter(0)

    def piece(self, level, part, index):
        start, width, _ = self.parts[part]
        if level < 2:
            size = self.held[level].shape[0] // 4
            return (aligned(index * size, size), pl.ds(start, width))
        cols = start + lax.rem(index, 2) * (width // 2)
        return (
            aligned(lax.div(index, 2) * 16, 16),
            pl.ds(pl.multiple_of(cols, LANES), width // 2),
        )

    def landing(self, level, part):
        start, width, _ = self.parts[part]
        if level < 2:
            return (slice(None), pl.ds(start, width))
        return (slice(None), pl.ds(start // 2, width // 2))

    def start_scatter(self, level):
        for part, (_, _, order) in enumerate(self.parts):
            axis = order[level]
            for k in (1, 2, 3):
                target = lax.rem(self.near.place(axis) + k, 4)
                copy = self.copy(
                    self.held[level].at[self.piece(level, part, target)],
                    self.incoming[level].at[(k - 1,) + self.landing(level, part)],
                    1 + (level * len(self.parts) + part) * 3 + k - 1,
                    self.near.at(axis, k),
                )
                copy.start()
                self.started.append(copy)
                self.copies[level, part, k] = copy

    def offset(self, part, levels):
        order = self.parts[part][2]
        row = self.base
        for level in range(levels):
            row = row + self.near.place(order[level]) * (self.half // 4 ** (level + 1))
        return row

    def final(self, part):
        start, width, order = self.parts[part]
        index = self.near.place(order[2])
        cols = start + lax.rem(index, 2) * (width // 2)
        rows = self.offset(part, 2) + lax.div(index, 2) * 16
        return (aligned(rows, 16), pl.ds(pl.multiple_of(cols, LANES), width // 2))

    def scatter(self, level):
        for part, (_, _, order) in enumerate(self.parts):
            for k in (1, 2, 3):
                self.copies[level, part, k].wait_recv()
            own = self.held[level][self.piece(level, part, self.near.place(order[level]))]
            total = own.astype(jnp.float32)
            for k in range(3):
                total += self.incoming[level][(k,) + self.landing(level, part)].astype(jnp.float32)
            total = total.astype(jnp.bfloat16)
            if level < 2:
                start, width, _ = self.parts[part]
                self.held[level + 1][:, start : start + width] = total
            else:
                self.full[self.final(part)] = total
        if level < 2:
            self.start_scatter(level + 1)
        else:
            self.start_gather(2)

    def gathered(self, level, part, step):
        start, width, order = self.parts[part]
        index = lax.rem(self.near.place(order[level]) + 4 - step, 4)
        if level == 2:
            cols = start + lax.rem(index, 2) * (width // 2)
            rows = self.offset(part, 2) + lax.div(index, 2) * 16
            return (aligned(rows, 16), pl.ds(pl.multiple_of(cols, LANES), width // 2))
        size = self.half // 4 ** (level + 1)
        rows = self.offset(part, level) + index * size
        return (aligned(rows, size), pl.ds(start, width))

    def start_gather(self, level):
        for part, (_, _, order) in enumerate(self.parts):
            for k in (1, 2, 3):
                slices = self.gathered(level, part, 0)
                copy = self.copy(
                    self.full.at[slices],
                    self.full.at[slices],
                    1 + ((3 + level) * len(self.parts) + part) * 3 + k - 1,
                    self.near.at(order[level], k),
                )
                copy.start()
                self.started.append(copy)

    def gather(self, level):
        for part, (_, _, order) in enumerate(self.parts):
            for k in (1, 2, 3):
                slices = self.gathered(level, part, k)
                self.copy(
                    self.full.at[slices],
                    self.full.at[slices],
                    1 + ((3 + level) * len(self.parts) + part) * 3 + k - 1,
                    self.near.at(order[level], k),
                ).wait_recv()
        if level > 0:
            self.start_gather(level - 1)

    def gather_pair(self):
        rows = aligned(self.base, self.half)
        copy = self.copy(
            self.full.at[rows], self.full.at[rows], 1 + 18 * len(self.parts), self.near.sibling
        )
        copy.start()
        self.started.append(copy)

    def gather_done(self):
        rows = aligned((1 - self.near.core) * self.half, self.half)
        self.copy(
            self.full.at[rows], self.full.at[rows], 1 + 18 * len(self.parts), self.near.sibling
        ).wait_recv()

    def sent(self):
        for copy in self.started:
            copy.wait_send()


def reduction_scratch(parts, width):
    half = width // 2
    kind = jnp.bfloat16
    slots = 2 + 18 * len(parts)
    return [
        pltpu.VMEM((width, width), kind),
        pltpu.VMEM((half, width), kind),
        pltpu.VMEM((half, width), kind),
        pltpu.VMEM((3, half // 4, width), kind),
        pltpu.VMEM((half // 4, width), kind),
        pltpu.VMEM((3, half // 16, width), kind),
        pltpu.VMEM((half // 16, width), kind),
        pltpu.VMEM((3, half // 32, width // 2), kind),
        pltpu.VMEM((width, width), kind),
        pltpu.SemaphoreType.DMA((slots,)),
        pltpu.SemaphoreType.DMA((slots,)),
    ]


def layer_kernel(
    n,
    document,
    summary,
    encoder_gain,
    memory_gain,
    summary_gain,
    query_weight,
    key_weight,
    value_weight,
    output_weight,
    cross_query,
    cross_key,
    cross_value,
    cross_output,
    encoder_cotangent,
    decoder_cotangent,
    encoded_out,
    decoded_out,
    own_out,
    cross_out,
    doc,
    states,
    weights,
    own_cotangent,
    cross_cotangent,
    normed,
    qkv_send,
    qkv_recv,
    sq_send,
    sq_recv,
    head_send,
    head_recv,
    kv_send,
    kv_recv,
    cross_send,
    cross_recv,
    value_low,
    value_high,
    encoded,
    decoded,
    load_sem,
    store_sem,
    send_sem,
    recv_sem,
    *grad_refs,
):
    dp = lax.axis_index("dp")
    me = lax.axis_index("ctx")
    rows = doc.shape[0]
    count = states.shape[0]
    width = doc.shape[1]
    blocks = width // (2 * LANES)

    loads = [
        pltpu.make_async_copy(src, dst, load_sem.at[i])
        for i, (src, dst) in enumerate(
            [
                (document, doc),
                (query_weight, weights.at[0]),
                (key_weight, weights.at[1]),
                (value_weight, weights.at[2]),
                (summary, states),
                (cross_query, weights.at[4]),
                (output_weight, weights.at[3]),
                (cross_key, weights.at[5]),
                (cross_value, weights.at[6]),
                (encoder_cotangent, own_cotangent),
                (cross_output, weights.at[7]),
                (decoder_cotangent, cross_cotangent),
            ]
        )
    ]
    for load in loads:
        load.start()

    near = Neighbours(dp, me)
    barrier = pltpu.get_barrier_semaphore()

    @pl.loop(1, n)
    def _(i):
        peer = lax.rem(me + i, n)
        pl.semaphore_signal(barrier, inc=1, device_id=(dp, peer), device_id_type=MESH)

    others = [near.sibling] + [near.at("x", k) for k in (1, 2, 3)] + [near.at("z", k) for k in (1, 3)]
    for device in others:
        pl.semaphore_signal(barrier, inc=1, device_id=device, device_id_type=MESH)

    def remote(phase, peer, source, src, dst):
        return pltpu.make_async_remote_copy(
            src_ref=src,
            dst_ref=dst,
            send_sem=send_sem.at[phase, peer],
            recv_sem=recv_sem.at[phase, source],
            device_id=(dp, peer),
            device_id_type=MESH,
        )

    def local(phase, src, dst):
        return pltpu.make_async_copy(src, dst, recv_sem.at[phase, me])

    def start(phase, peer, src, dst):
        @pl.when(peer != me)
        def _():
            remote(phase, peer, me, src, dst).start()

        @pl.when(peer == me)
        def _():
            local(phase, src, dst).start()

    def wait_all(phase, src_of, dst_of):
        @pl.loop(0, n)
        def _(source):
            @pl.when(source != me)
            def _():
                remote(phase, source, source, src_of(source), dst_of(source)).wait_recv()

            @pl.when(source == me)
            def _():
                local(phase, src_of(source), dst_of(source)).wait()

    def wait_sent(phase, src_of, dst_of):
        @pl.loop(0, n)
        def _(peer):
            @pl.when(peer != me)
            def _():
                remote(phase, peer, me, src_of(peer), dst_of(peer)).wait_send()

    def column(index):
        return pl.ds(pl.multiple_of(index * LANES, LANES), LANES)

    def wide(index):
        return pl.ds(pl.multiple_of(index * 2 * LANES, 2 * LANES), 2 * LANES)

    loads[0].wait()
    normed[...] = norm_rows(doc[...], encoder_gain[...])
    for i in (1, 2, 3):
        loads[i].wait()
    pl.semaphore_wait(barrier, n - 1 + len(others))

    @pl.loop(0, blocks)
    def _(i):
        block = lax.rem(lax.div(me, 2) + (blocks - 1) - i, blocks)
        for t in range(3):
            part = matmul(normed[...], weights[t, :, wide(block)]).astype(jnp.bfloat16)
            qkv_send[2 * block, t] = part[:, :LANES]
            qkv_send[2 * block + 1, t] = part[:, LANES:]
        for half in range(2):
            peer = 2 * block + half
            start(QKV, peer, qkv_send.at[peer], qkv_recv.at[:, me])

    loads[4].wait()
    loads[5].wait()
    normed[0:count, :] = norm_rows(states[...], summary_gain[...])

    @pl.loop(0, blocks)
    def _(i):
        block = lax.rem(lax.div(me, 2) + (blocks - 1) - i, blocks)
        part = matmul(normed[0:count, :], weights[4, :, wide(block)]).astype(jnp.bfloat16)
        sq_send[2 * block] = part[:, :LANES]
        sq_send[2 * block + 1] = part[:, LANES:]
        for half in range(2):
            peer = 2 * block + half
            start(SQ, peer, sq_send.at[peer], sq_recv.at[me])

    lane = lax.broadcasted_iota(jnp.int32, (1, LANES), 1)
    low = lane < HEAD_DIM
    zero = jnp.zeros((), jnp.bfloat16)
    one = jnp.ones((), jnp.bfloat16)

    def set_values(ref):
        values = ref[...].reshape(n * rows, LANES)
        value_low[...] = jnp.where(low, values, one)
        value_high[...] = jnp.where(low, one, values)

    def attend(query, keys):
        def head(part, values):
            scores = lax.dot_general(
                part, keys, (((1,), (1,)), ((), ())), preferred_element_type=jnp.float32
            )
            top = jnp.max(scores, axis=-1, keepdims=True)
            weight = jnp.exp(scores - top).astype(jnp.bfloat16)
            return matmul(weight, values[...])

        left = head(jnp.where(low, query, zero), value_low)
        right = head(jnp.where(low, zero, query), value_high)
        mixed = jnp.where(low, left, right)
        total = jnp.where(
            low, pltpu.roll(left, HEAD_DIM, 1), pltpu.roll(right, HEAD_DIM, 1)
        )
        return (mixed / total).astype(jnp.bfloat16)

    wait_all(QKV, lambda s: qkv_send.at[s], lambda s: qkv_recv.at[:, s])
    set_values(qkv_recv.at[2])

    @pl.loop(0, n)
    def _(i):
        peer = lax.rem(me + 1 + i, n)
        keys = qkv_recv[1].reshape(n * rows, LANES)
        head_send[peer] = attend(qkv_recv[0, peer], keys)
        start(HEAD, peer, head_send.at[peer], head_recv.at[:, column(me)])

    loads[6].wait()
    wait_all(HEAD, lambda s: head_send.at[s], lambda s: head_recv.at[:, column(s)])

    @pl.loop(0, blocks)
    def _(i):
        mixed = matmul(head_recv[...], weights[3, :, wide(i)])
        encoded[:, wide(i)] = (doc[:, wide(i)].astype(jnp.float32) + mixed).astype(jnp.bfloat16)

    own_refs = Reduction(near, OWN_PARTS, *grad_refs[:REFS])
    cross_refs = Reduction(near, CROSS_PARTS, *grad_refs[REFS:])
    stores = [
        pltpu.make_async_copy(src, dst, store_sem.at[i])
        for i, (src, dst) in enumerate(
            [
                (encoded, encoded_out),
                (decoded, decoded_out),
                (own_refs.full, own_out),
                (cross_refs.full, cross_out),
            ]
        )
    ]
    stores[0].start()

    normed[...] = norm_rows(encoded[...], memory_gain[...])
    loads[7].wait()
    loads[8].wait()

    @pl.loop(0, blocks)
    def _(i):
        block = lax.rem(lax.div(me, 2) + (blocks - 1) - i, blocks)
        for t in range(2):
            part = matmul(normed[...], weights[5 + t, :, wide(block)]).astype(jnp.bfloat16)
            kv_send[2 * block, t] = part[:, :LANES]
            kv_send[2 * block + 1, t] = part[:, LANES:]
        for half in range(2):
            peer = 2 * block + half
            start(KV, peer, kv_send.at[peer], kv_recv.at[:, me])

    loads[9].wait()
    own_refs.product(head_recv, own_cotangent)
    own_refs.pair_sum()

    wait_all(SQ, lambda s: sq_send.at[s], lambda s: sq_recv.at[s])
    wait_all(KV, lambda s: kv_send.at[s], lambda s: kv_recv.at[:, s])
    set_values(kv_recv.at[1])

    @pl.loop(0, n // 2)
    def _(i):
        pair = lax.rem(lax.div(me, 2) + 1 + i, n // 2)
        keys = kv_recv[0].reshape(n * rows, LANES)
        query = sq_recv[pl.ds(2 * pair, 2)].reshape(2 * count, LANES)
        mixed = attend(query, keys)
        cross_send[2 * pair] = mixed[:count]
        cross_send[2 * pair + 1] = mixed[count:]
        for half in range(2):
            peer = 2 * pair + half
            start(CROSS, peer, cross_send.at[peer], cross_recv.at[:, column(me)])

    own_refs.scatter(0)
    loads[11].wait()
    wait_all(CROSS, lambda s: cross_send.at[s], lambda s: cross_recv.at[:, column(s)])
    cross_refs.product(cross_recv, cross_cotangent)
    loads[10].wait()

    @pl.loop(0, blocks)
    def _(i):
        mixed = matmul(cross_recv[...], weights[7, :, wide(i)])
        decoded[:, wide(i)] = (states[:, wide(i)].astype(jnp.float32) + mixed).astype(jnp.bfloat16)

    stores[1].start()
    cross_refs.pair_sum()
    own_refs.scatter(1)
    cross_refs.scatter(0)
    own_refs.scatter(2)
    cross_refs.scatter(1)
    own_refs.gather(2)
    cross_refs.scatter(2)
    own_refs.gather(1)
    cross_refs.gather(2)
    own_refs.gather(0)
    cross_refs.gather(1)
    own_refs.gather_pair()
    cross_refs.gather(0)
    own_refs.gather_done()
    stores[2].start()
    cross_refs.gather_pair()
    cross_refs.gather_done()
    stores[3].start()
    wait_sent(QKV, lambda p: qkv_send.at[p], lambda p: qkv_recv.at[:, me])
    wait_sent(SQ, lambda p: sq_send.at[p], lambda p: sq_recv.at[me])
    wait_sent(HEAD, lambda p: head_send.at[p], lambda p: head_recv.at[:, column(me)])
    wait_sent(KV, lambda p: kv_send.at[p], lambda p: kv_recv.at[:, me])
    wait_sent(CROSS, lambda p: cross_send.at[p], lambda p: cross_recv.at[:, column(me)])
    own_refs.sent()
    cross_refs.sent()
    for store in stores:
        store.wait()


def solution(mesh):
    n = mesh.shape["ctx"]

    def body(
        document,
        summary,
        encoder_gain,
        query_weight,
        key_weight,
        value_weight,
        output_weight,
        memory_gain,
        summary_gain,
        cross_query,
        cross_key,
        cross_value,
        cross_output,
        encoder_cotangent,
        decoder_cotangent,
    ):
        rows, width = document.shape[1:]
        count = summary.shape[1]
        half = jnp.bfloat16
        hbm = pl.BlockSpec(memory_space=pl.ANY)
        vmem = pl.BlockSpec(memory_space=pltpu.VMEM)
        encoded, decoded, own_grad, cross_grad = pl.pallas_call(
            functools.partial(layer_kernel, n),
            out_shape=[
                jax.ShapeDtypeStruct((rows, width), half),
                jax.ShapeDtypeStruct((count, width), half),
                jax.ShapeDtypeStruct((width, width), half),
                jax.ShapeDtypeStruct((width, width), half),
            ],
            in_specs=[hbm] * 2 + [vmem] * 3 + [hbm] * 10,
            out_specs=[hbm] * 4,
            scratch_shapes=[
                pltpu.VMEM((rows, width), half),
                pltpu.VMEM((count, width), half),
                pltpu.VMEM((8, width, width), half),
                pltpu.VMEM((rows, width), half),
                pltpu.VMEM((count, width), half),
                pltpu.VMEM((rows, width), half),
                pltpu.VMEM((n, 3, rows, LANES), half),
                pltpu.VMEM((3, n, rows, LANES), half),
                pltpu.VMEM((n, count, LANES), half),
                pltpu.VMEM((n, count, LANES), half),
                pltpu.VMEM((n, rows, LANES), half),
                pltpu.VMEM((rows, width), half),
                pltpu.VMEM((n, 2, rows, LANES), half),
                pltpu.VMEM((2, n, rows, LANES), half),
                pltpu.VMEM((n, count, LANES), half),
                pltpu.VMEM((count, width), half),
                pltpu.VMEM((n * rows, LANES), half),
                pltpu.VMEM((n * rows, LANES), half),
                pltpu.VMEM((rows, width), half),
                pltpu.VMEM((count, width), half),
                pltpu.SemaphoreType.DMA((12,)),
                pltpu.SemaphoreType.DMA((4,)),
                pltpu.SemaphoreType.DMA((5, n)),
                pltpu.SemaphoreType.DMA((5, n)),
                *reduction_scratch(OWN_PARTS, width),
                *reduction_scratch(CROSS_PARTS, width),
            ],
            compiler_params=pltpu.CompilerParams(
                collective_id=0, has_side_effects=True, vmem_limit_bytes=56 * 2**20
            ),
        )(
            document[0],
            summary[0],
            encoder_gain[None],
            memory_gain[None],
            summary_gain[None],
            query_weight,
            key_weight,
            value_weight,
            output_weight,
            cross_query,
            cross_key,
            cross_value,
            cross_output,
            encoder_cotangent[0],
            decoder_cotangent[0],
        )
        return (
            encoded[None],
            decoded[None],
            own_grad,
            cross_grad,
        )

    rows_spec = P("dp", "ctx", None)
    return jax.shard_map(
        body,
        mesh=mesh,
        in_specs=(rows_spec, rows_spec) + (P(),) * 11 + (rows_spec, rows_spec),
        out_specs=(rows_spec, rows_spec, P(), P()),
        check_vma=False,
    )
```

```python
import functools

import jax
import jax.numpy as jnp
from jax import lax
from jax.experimental import pallas as pl
from jax.experimental.pallas import tpu as pltpu
from jax.sharding import PartitionSpec as P

HEADS = 16
HEAD_DIM = 64
LANES = 128
MESH = pl.DeviceIdType.MESH
SELF_KV, SELF_Q, SQ, HEAD, KV, CROSS = range(6)


def norm_rows(rows, gain):
    values = rows.astype(jnp.float32)
    scale = lax.rsqrt(jnp.mean(values * values, axis=-1, keepdims=True) + 1e-06)
    return (values * scale * gain).astype(jnp.bfloat16)


def matmul(left, right):
    return jnp.dot(left, right, preferred_element_type=jnp.float32)


OWN_PARTS = ((0, 1024, "x"),)
CROSS_PARTS = ((0, 512, "y"), (512, 512, "z"))
REFS = 8


class Neighbours:
    def __init__(self, dp, ctx):
        self.core = lax.rem(dp, 2)
        self.x = lax.div(dp, 4)
        self.y = lax.rem(ctx, 4)
        self.z = lax.div(ctx, 4) * 2 + lax.rem(lax.div(dp, 2), 2)
        self.sibling = self.device(self.x, self.y, self.z, 1 - self.core)

    def device(self, x, y, z, core):
        return (x * 4 + lax.rem(z, 2) * 2 + core, lax.div(z, 2) * 4 + y)

    def place(self, axis):
        return {"x": self.x, "y": self.y, "z": self.z}[axis]

    def step(self, **steps):
        place = {"x": self.x, "y": self.y, "z": self.z}
        for axis, step in steps.items():
            place[axis] = lax.rem(place[axis] + step, 4)
        return self.device(place["x"], place["y"], place["z"], self.core)

    def distant(self):
        steps = [(i, j, k) for i in range(4) for j in range(4) for k in range(4)]
        steps = [(i, j, k) for i, j, k in steps if 0 in (i, j, k) and (i > 0 or k % 2 == 1)]
        return [self.sibling] + [self.step(x=i, y=j, z=k) for i, j, k in steps]


def aligned(start, size):
    return pl.ds(pl.multiple_of(start, size), size)


def grid_of(width):
    across = min(4, width // LANES)
    return across, 128 * across // 16, width // across


class Reduction:
    def __init__(
        self, near, parts, full, partial, pair, first, first_in, second, second_in, send, recv
    ):
        self.near = near
        self.parts = parts
        self.partial, self.pair, self.full = partial, pair, full
        self.first, self.first_in = first, first_in
        self.second, self.second_in = second, second_in
        self.send, self.recv = send, recv
        self.half = pair.shape[0]
        self.base = near.core * self.half
        self.slot = 0
        self.started = []
        self.copies = {}

    def copy(self, key, src, dst, device):
        slot = len(self.copies)
        self.copies[key] = pltpu.make_async_remote_copy(
            src_ref=src,
            dst_ref=dst,
            send_sem=self.send.at[slot],
            recv_sem=self.recv.at[slot],
            device_id=device,
            device_id_type=MESH,
        )
        self.copies[key].start()

    def arrived(self, key, dst):
        slot = list(self.copies).index(key)
        pltpu.make_async_remote_copy(
            src_ref=dst,
            dst_ref=dst,
            send_sem=self.send.at[slot],
            recv_sem=self.recv.at[slot],
            device_id=self.near.sibling,
            device_id_type=MESH,
        ).wait_recv()

    def product(self, left, right):
        step = 256
        for side in (1, 0):
            start = self.base if side == 0 else (1 - self.near.core) * self.half
            for i in range(self.half // step):
                rows = aligned(start + i * step, step)
                mixed = lax.dot_general(
                    left[:, rows],
                    right[...],
                    (((0,), (0,)), ((), ())),
                    preferred_element_type=jnp.float32,
                )
                self.partial[rows, :] = mixed.astype(jnp.bfloat16)
                if side == 1:
                    block = pl.ds(i * step, step)
                    self.copy(
                        ("pair", i), self.partial.at[rows], self.pair.at[block], self.near.sibling
                    )

    def pair_sum(self):
        step = 256
        for i in range(self.half // step):
            block = pl.ds(i * step, step)
            self.arrived(("pair", i), self.pair.at[block])
            own = self.partial[aligned(self.base + i * step, step), :].astype(jnp.float32)
            total = own + self.pair[block, :].astype(jnp.float32)
            self.first[block, :] = total.astype(jnp.bfloat16)
        size = self.half // 4
        for k in (2, 1, 3):
            for part, (start, width, axis) in enumerate(self.parts):
                target = lax.rem(self.near.place(axis) + k, 4)
                cols = pl.ds(start, width)
                self.copy(
                    ("first", part, k),
                    self.first.at[aligned(target * size, size), cols],
                    self.first_in.at[k - 1, :, cols],
                    self.near.step(**{axis: k}),
                )

    def rest(self, part):
        one, two = [axis for axis in "xyz" if axis != self.parts[part][2]]
        for i in range(4):
            for j in range(4):
                if i or j:
                    yield i * 4 + j, {one: i, two: j}

    def index(self, part, steps={}):
        one, two = [axis for axis in "xyz" if axis != self.parts[part][2]]
        a = lax.rem(self.near.place(one) + steps.get(one, 0), 4)
        b = lax.rem(self.near.place(two) + steps.get(two, 0), 4)
        return a * 4 + b

    def piece(self, part, index, base=0):
        start, width, _ = self.parts[part]
        across, rows, cols = grid_of(width)
        row = lax.div(index, across) * rows + base
        col = start + lax.rem(index, across) * cols
        return (aligned(row, rows), pl.ds(pl.multiple_of(col, LANES), cols))

    def landing(self, part, k):
        start, width, _ = self.parts[part]
        _, rows, cols = grid_of(width)
        return (k - 1, pl.ds(0, rows), pl.ds(part * LANES, cols))

    def scatter_first(self):
        size = self.half // 4
        for part, (start, width, axis) in enumerate(self.parts):
            cols = pl.ds(start, width)
            total = self.first[aligned(self.near.place(axis) * size, size), cols].astype(jnp.float32)
            for k in (1, 3, 2):
                place = self.first_in.at[k - 1, :, cols]
                self.arrived(("first", part, k), place)
                total += place[...].astype(jnp.float32)
            self.second[:, cols] = total.astype(jnp.bfloat16)
            for k, steps in self.rest(part):
                self.copy(
                    ("second", part, k),
                    self.second.at[self.piece(part, self.index(part, steps))],
                    self.second_in.at[self.landing(part, k)],
                    self.near.step(**steps),
                )

    def own_rows(self, part, step=0):
        place = lax.rem(self.near.place(self.parts[part][2]) + 4 - step, 4)
        return self.base + place * (self.half // 4)

    def scatter_second(self):
        for part in range(len(self.parts)):
            total = self.second[self.piece(part, self.index(part))].astype(jnp.float32)
            for k, _ in self.rest(part):
                place = self.second_in.at[self.landing(part, k)]
                self.arrived(("second", part, k), place)
                total += place[...].astype(jnp.float32)
            slices = self.piece(part, self.index(part), self.own_rows(part))
            self.full[slices] = total.astype(jnp.bfloat16)
            for k, steps in self.rest(part):
                place = self.full.at[slices]
                self.copy(("back", part, k), place, place, self.near.step(**steps))

    def gather_second(self):
        size = self.half // 4
        for part, (start, width, axis) in enumerate(self.parts):
            for k, steps in self.rest(part):
                behind = {name: 4 - step for name, step in steps.items()}
                slices = self.piece(part, self.index(part, behind), self.own_rows(part))
                self.arrived(("back", part, k), self.full.at[slices])
            place = self.full.at[aligned(self.own_rows(part), size), pl.ds(start, width)]
            for k in (2, 1, 3):
                self.copy(("last", part, k), place, place, self.near.step(**{axis: k}))
            self.copy(("across", part, 0), place, place, self.near.sibling)

    def gather_first(self):
        size = self.half // 4
        for k in (1, 3, 2):
            for part, (start, width, axis) in enumerate(self.parts):
                rows = aligned(self.own_rows(part, k), size)
                place = self.full.at[rows, pl.ds(start, width)]
                self.arrived(("last", part, k), place)
                self.copy(("across", part, k), place, place, self.near.sibling)

    def finish(self):
        size = self.half // 4
        for part, (start, width, axis) in enumerate(self.parts):
            for k in range(4):
                rows = aligned(
                    self.own_rows(part, k) + (1 - 2 * self.near.core) * self.half, size
                )
                self.arrived(("across", part, k), self.full.at[rows, pl.ds(start, width)])
        for copy in self.copies.values():
            copy.wait_send()


def reduction_scratch(parts, width):
    half = width // 2
    kind = jnp.bfloat16
    slots = 2 + 40 * len(parts)
    return [
        pltpu.VMEM((width, width), kind),
        pltpu.VMEM((half, width), kind),
        pltpu.VMEM((half, width), kind),
        pltpu.VMEM((3, half // 4, width), kind),
        pltpu.VMEM((half // 4, width), kind),
        pltpu.VMEM((15, half // 16, width // 2), kind),
        pltpu.SemaphoreType.DMA((slots,)),
        pltpu.SemaphoreType.DMA((slots,)),
    ]


def layer_kernel(
    n,
    document,
    summary,
    encoder_gain,
    memory_gain,
    summary_gain,
    query_weight,
    key_weight,
    value_weight,
    output_weight,
    cross_query,
    cross_key,
    cross_value,
    cross_output,
    encoder_cotangent,
    decoder_cotangent,
    encoded,
    decoded,
    own_full,
    cross_full,
    doc,
    states,
    weights,
    own_cotangent,
    cross_cotangent,
    normed,
    qkv_send,
    qkv_recv,
    sq_send,
    sq_recv,
    head_send,
    head_recv,
    kv_send,
    kv_recv,
    cross_send,
    cross_recv,
    value_low,
    value_high,
    load_sem,
    send_sem,
    recv_sem,
    *grad_refs,
):
    dp = lax.axis_index("dp")
    me = lax.axis_index("ctx")
    rows = doc.shape[0]
    count = states.shape[0]
    width = doc.shape[1]
    blocks = width // (2 * LANES)

    loads = [
        pltpu.make_async_copy(src, dst, load_sem.at[i])
        for i, (src, dst) in enumerate(
            [
                (document, doc),
                (query_weight, weights.at[0]),
                (key_weight, weights.at[1]),
                (value_weight, weights.at[2]),
                (summary, states),
                (cross_query, weights.at[4]),
                (output_weight, weights.at[3]),
                (cross_key, weights.at[5]),
                (cross_value, weights.at[6]),
                (encoder_cotangent, own_cotangent),
                (cross_output, weights.at[7]),
                (decoder_cotangent, cross_cotangent),
            ]
        )
    ]
    for i in (0, 2, 3, 1, 4, 5, 6, 7, 8, 9, 10, 11):
        loads[i].start()

    near = Neighbours(dp, me)
    barrier = pltpu.get_barrier_semaphore()

    @pl.loop(1, n)
    def _(i):
        peer = lax.rem(me + i, n)
        pl.semaphore_signal(barrier, inc=1, device_id=(dp, peer), device_id_type=MESH)

    others = near.distant()
    for device in others:
        pl.semaphore_signal(barrier, inc=1, device_id=device, device_id_type=MESH)

    def remote(phase, peer, source, src, dst):
        return pltpu.make_async_remote_copy(
            src_ref=src,
            dst_ref=dst,
            send_sem=send_sem.at[phase, peer],
            recv_sem=recv_sem.at[phase, source],
            device_id=(dp, peer),
            device_id_type=MESH,
        )

    def local(phase, src, dst):
        return pltpu.make_async_copy(src, dst, recv_sem.at[phase, me])

    def start(phase, peer, src, dst):
        @pl.when(peer != me)
        def _():
            remote(phase, peer, me, src, dst).start()

        @pl.when(peer == me)
        def _():
            local(phase, src, dst).start()

    def wait_one(phase, source, src, dst):
        @pl.when(source != me)
        def _():
            remote(phase, source, source, src, dst).wait_recv()

        @pl.when(source == me)
        def _():
            local(phase, src, dst).wait()

    def wait_all(phase, src_of, dst_of):
        @pl.loop(0, n)
        def _(source):
            wait_one(phase, source, src_of(source), dst_of(source))

    def wait_sent(phase, src_of, dst_of):
        @pl.loop(0, n)
        def _(peer):
            @pl.when(peer != me)
            def _():
                remote(phase, peer, me, src_of(peer), dst_of(peer)).wait_send()

    def column(index):
        return pl.ds(pl.multiple_of(index * LANES, LANES), LANES)

    def wide(index):
        return pl.ds(pl.multiple_of(index * 2 * LANES, 2 * LANES), 2 * LANES)

    loads[0].wait()
    normed[...] = norm_rows(doc[...], encoder_gain[...])
    pl.semaphore_wait(barrier, n - 1 + len(others))
    loads[2].wait()
    loads[3].wait()

    @pl.loop(0, blocks)
    def _(i):
        block = lax.rem(lax.div(me, 2) + (blocks - 1) - i, blocks)
        for t in (1, 2):
            part = matmul(normed[...], weights[t, :, wide(block)]).astype(jnp.bfloat16)
            qkv_send[2 * block, t] = part[:, :LANES]
            qkv_send[2 * block + 1, t] = part[:, LANES:]
        for half in range(2):
            peer = 2 * block + half
            start(SELF_KV, peer, qkv_send.at[peer, pl.ds(1, 2)], qkv_recv.at[pl.ds(1, 2), me])

    loads[1].wait()

    @pl.loop(0, blocks)
    def _(i):
        part = matmul(normed[...], weights[0, :, wide(i)]).astype(jnp.bfloat16)
        qkv_send[2 * i, 0] = part[:, :LANES]
        qkv_send[2 * i + 1, 0] = part[:, LANES:]

    loads[4].wait()
    loads[5].wait()
    normed[0:count, :] = norm_rows(states[...], summary_gain[...])

    @pl.loop(0, blocks)
    def _(i):
        part = matmul(normed[0:count, :], weights[4, :, wide(i)]).astype(jnp.bfloat16)
        sq_send[2 * i] = part[:, :LANES]
        sq_send[2 * i + 1] = part[:, LANES:]

    kv_sent = lambda p: qkv_send.at[p, pl.ds(1, 2)], lambda p: qkv_recv.at[pl.ds(1, 2), me]
    wait_sent(SELF_KV, *kv_sent)

    @pl.loop(0, n)
    def _(i):
        peer = lax.rem(me + n - i, n)
        start(SELF_Q, peer, qkv_send.at[peer, 0], qkv_recv.at[0, me])

    lane = lax.broadcasted_iota(jnp.int32, (1, LANES), 1)
    low = lane < HEAD_DIM
    zero = jnp.zeros((), jnp.bfloat16)
    one = jnp.ones((), jnp.bfloat16)

    def set_values(ref):
        values = ref[...].reshape(n * rows, LANES)
        value_low[...] = jnp.where(low, values, one)
        value_high[...] = jnp.where(low, one, values)

    def attend(query, keys):
        def head(part, values):
            scores = lax.dot_general(
                part, keys, (((1,), (1,)), ((), ())), preferred_element_type=jnp.float32
            )
            top = jnp.max(scores, axis=-1, keepdims=True)
            weight = jnp.exp(scores - top).astype(jnp.bfloat16)
            return matmul(weight, values[...])

        left = head(jnp.where(low, query, zero), value_low)
        right = head(jnp.where(low, zero, query), value_high)
        mixed = jnp.where(low, left, right)
        total = jnp.where(
            low, pltpu.roll(left, HEAD_DIM, 1), pltpu.roll(right, HEAD_DIM, 1)
        )
        return (mixed / total).astype(jnp.bfloat16)

    wait_all(
        SELF_KV, lambda s: qkv_send.at[s, pl.ds(1, 2)], lambda s: qkv_recv.at[pl.ds(1, 2), s]
    )
    set_values(qkv_recv.at[2])

    @pl.loop(0, n)
    def _(i):
        peer = lax.rem(me + i, n)
        wait_one(SELF_Q, peer, qkv_send.at[peer, 0], qkv_recv.at[0, peer])
        keys = qkv_recv[1].reshape(n * rows, LANES)
        head_send[peer] = attend(qkv_recv[0, peer], keys)
        start(HEAD, peer, head_send.at[peer], head_recv.at[:, column(me)])

        @pl.when(i == 2)
        def _():
            @pl.loop(0, n)
            def _(p):
                start(SQ, p, sq_send.at[p], sq_recv.at[me])

    loads[6].wait()
    wait_all(HEAD, lambda s: head_send.at[s], lambda s: head_recv.at[:, column(s)])

    @pl.loop(0, blocks)
    def _(i):
        mixed = matmul(head_recv[...], weights[3, :, wide(i)])
        encoded[:, wide(i)] = (doc[:, wide(i)].astype(jnp.float32) + mixed).astype(jnp.bfloat16)

    own_refs = Reduction(near, OWN_PARTS, own_full, *grad_refs[:REFS])
    cross_refs = Reduction(near, CROSS_PARTS, cross_full, *grad_refs[REFS:])

    normed[...] = norm_rows(encoded[...], memory_gain[...])
    loads[7].wait()
    loads[8].wait()

    @pl.loop(0, blocks)
    def _(i):
        block = lax.rem(lax.div(me, 2) + (blocks - 1) - i, blocks)
        for t in range(2):
            part = matmul(normed[...], weights[5 + t, :, wide(block)]).astype(jnp.bfloat16)
            kv_send[2 * block, t] = part[:, :LANES]
            kv_send[2 * block + 1, t] = part[:, LANES:]
        for half in range(2):
            peer = 2 * block + half
            start(KV, peer, kv_send.at[peer], kv_recv.at[:, me])

    loads[9].wait()
    own_refs.product(head_recv, own_cotangent)
    own_refs.pair_sum()

    wait_all(SQ, lambda s: sq_send.at[s], lambda s: sq_recv.at[s])
    wait_all(KV, lambda s: kv_send.at[s], lambda s: kv_recv.at[:, s])
    set_values(kv_recv.at[1])

    @pl.loop(0, n // 2)
    def _(i):
        pair = lax.rem(lax.div(me, 2) + 1 + i, n // 2)
        keys = kv_recv[0].reshape(n * rows, LANES)
        query = sq_recv[pl.ds(2 * pair, 2)].reshape(2 * count, LANES)
        mixed = attend(query, keys)
        cross_send[2 * pair] = mixed[:count]
        cross_send[2 * pair + 1] = mixed[count:]
        for half in range(2):
            peer = 2 * pair + half
            start(CROSS, peer, cross_send.at[peer], cross_recv.at[:, column(me)])

    loads[11].wait()
    wait_all(CROSS, lambda s: cross_send.at[s], lambda s: cross_recv.at[:, column(s)])
    cross_refs.product(cross_recv, cross_cotangent)
    own_refs.scatter_first()
    cross_refs.pair_sum()
    loads[10].wait()

    @pl.loop(0, blocks)
    def _(i):
        mixed = matmul(cross_recv[...], weights[7, :, wide(i)])
        decoded[:, wide(i)] = (states[:, wide(i)].astype(jnp.float32) + mixed).astype(jnp.bfloat16)

    own_refs.scatter_second()
    cross_refs.scatter_first()
    own_refs.gather_second()
    cross_refs.scatter_second()
    cross_refs.gather_second()
    own_refs.gather_first()
    cross_refs.gather_first()
    own_refs.finish()
    cross_refs.finish()
    wait_sent(SELF_Q, lambda p: qkv_send.at[p, 0], lambda p: qkv_recv.at[0, me])
    wait_sent(SQ, lambda p: sq_send.at[p], lambda p: sq_recv.at[me])
    wait_sent(HEAD, lambda p: head_send.at[p], lambda p: head_recv.at[:, column(me)])
    wait_sent(KV, lambda p: kv_send.at[p], lambda p: kv_recv.at[:, me])
    wait_sent(CROSS, lambda p: cross_send.at[p], lambda p: cross_recv.at[:, column(me)])


def solution(mesh):
    n = mesh.shape["ctx"]

    def body(
        document,
        summary,
        encoder_gain,
        query_weight,
        key_weight,
        value_weight,
        output_weight,
        memory_gain,
        summary_gain,
        cross_query,
        cross_key,
        cross_value,
        cross_output,
        encoder_cotangent,
        decoder_cotangent,
    ):
        rows, width = document.shape[1:]
        count = summary.shape[1]
        half = jnp.bfloat16
        hbm = pl.BlockSpec(memory_space=pl.ANY)
        vmem = pl.BlockSpec(memory_space=pltpu.VMEM)
        shapes = [(rows, width), (count, width), (width, width), (width, width)]
        encoded, decoded, own_grad, cross_grad = pl.pallas_call(
            functools.partial(layer_kernel, n),
            out_shape=[pltpu.VMEM(shape, half) for shape in shapes],
            in_specs=[hbm] * 2 + [vmem] * 3 + [hbm] * 10,
            out_specs=[vmem] * 4,
            scratch_shapes=[
                pltpu.VMEM((rows, width), half),
                pltpu.VMEM((count, width), half),
                pltpu.VMEM((8, width, width), half),
                pltpu.VMEM((rows, width), half),
                pltpu.VMEM((count, width), half),
                pltpu.VMEM((rows, width), half),
                pltpu.VMEM((n, 3, rows, LANES), half),
                pltpu.VMEM((3, n, rows, LANES), half),
                pltpu.VMEM((n, count, LANES), half),
                pltpu.VMEM((n, count, LANES), half),
                pltpu.VMEM((n, rows, LANES), half),
                pltpu.VMEM((rows, width), half),
                pltpu.VMEM((n, 2, rows, LANES), half),
                pltpu.VMEM((2, n, rows, LANES), half),
                pltpu.VMEM((n, count, LANES), half),
                pltpu.VMEM((count, width), half),
                pltpu.VMEM((n * rows, LANES), half),
                pltpu.VMEM((n * rows, LANES), half),
                pltpu.SemaphoreType.DMA((12,)),
                pltpu.SemaphoreType.DMA((6, n)),
                pltpu.SemaphoreType.DMA((6, n)),
                *reduction_scratch(OWN_PARTS, width),
                *reduction_scratch(CROSS_PARTS, width),
            ],
            compiler_params=pltpu.CompilerParams(
                collective_id=0, has_side_effects=True, vmem_limit_bytes=50 * 2**20
            ),
        )(
            document[0],
            summary[0],
            encoder_gain[None],
            memory_gain[None],
            summary_gain[None],
            query_weight,
            key_weight,
            value_weight,
            output_weight,
            cross_query,
            cross_key,
            cross_value,
            cross_output,
            encoder_cotangent[0],
            decoder_cotangent[0],
        )
        return (
            encoded[None],
            decoded[None],
            own_grad,
            cross_grad,
        )

    rows_spec = P("dp", "ctx", None)
    return jax.shard_map(
        body,
        mesh=mesh,
        in_specs=(rows_spec, rows_spec) + (P(),) * 11 + (rows_spec, rows_spec),
        out_specs=(rows_spec, rows_spec, P(), P()),
        check_vma=False,
    )
```

```python
import functools

import jax
import jax.numpy as jnp
from jax import lax
from jax.experimental import pallas as pl
from jax.experimental.pallas import tpu as pltpu
from jax.sharding import PartitionSpec as P

HEADS = 16
HEAD_DIM = 64
LANES = 128
MESH = pl.DeviceIdType.MESH
SELF_KV, SELF_Q, SQ, HEAD, KV, CROSS = range(6)


def norm_rows(rows, gain):
    values = rows.astype(jnp.float32)
    scale = lax.rsqrt(jnp.mean(values * values, axis=-1, keepdims=True) + 1e-06)
    return (values * scale * gain).astype(jnp.bfloat16)


def matmul(left, right):
    return jnp.dot(left, right, preferred_element_type=jnp.float32)


OWN_PARTS = ((0, 1024, "x"),)
CROSS_PARTS = ((0, 512, "y"), (512, 256, "z"), (768, 256, "x"))
REFS = 8


class Neighbours:
    def __init__(self, dp, ctx):
        self.core = dp & 1
        low, high = (dp >> 1) & 1, ctx >> 2
        place = {"x": dp >> 2, "y": ctx & 3, "z": high * 2 + low}
        self.places = {axis: [(start + k) & 3 for k in range(4)] for axis, start in place.items()}
        self.dp_x = [x * 4 for x in self.places["x"]]
        self.dp_z = [(z & 1) * 2 + self.core for z in self.places["z"]]
        self.ctx_z = [(z >> 1) * 4 for z in self.places["z"]]
        self.sibling = (dp + 1 - 2 * self.core, ctx)

    def step(self, x=0, y=0, z=0):
        return (self.dp_x[x] + self.dp_z[z], self.ctx_z[z] + self.places["y"][y])

    def distant(self):
        parts = OWN_PARTS + CROSS_PARTS
        reached = {tuple(k if axis == name else 0 for name in "xyz") for *_, axis in parts for k in (1, 2, 3)}
        for *_, axis in parts:
            for steps in rest(axis):
                reached.add(tuple(steps.get(name, 0) for name in "xyz"))
        reached = sorted((i, j, k) for i, j, k in reached if i > 0 or k % 2 == 1)
        return [self.sibling] + [self.step(*steps) for steps in reached]


def rest(axis):
    one, two = [name for name in "xyz" if name != axis]
    return [{one: i, two: j} for i in range(4) for j in range(4) if i or j]


def aligned(start, size):
    return pl.ds(pl.multiple_of(start, size), size)


class Reduction:
    def __init__(
        self, near, parts, full, partial, pair, first, first_in, second, second_in, send, recv
    ):
        self.near = near
        self.parts = parts
        self.partial, self.pair, self.full = partial, pair, full
        self.first, self.first_in = first, first_in
        self.second, self.second_in = second, second_in
        self.send, self.recv = send, recv
        self.half = pair.shape[0]
        self.size = self.half // 4
        self.base = near.core * self.half
        self.other = self.half - self.base
        self.slots = {}

    def copy(self, key, src, dst, device):
        slot = self.slots.setdefault(key, len(self.slots))
        return pltpu.make_async_remote_copy(
            src_ref=src,
            dst_ref=dst,
            send_sem=self.send.at[slot],
            recv_sem=self.recv.at[slot],
            device_id=device,
            device_id_type=MESH,
        )

    def arrived(self, key, place):
        self.copy(key, place, place, self.near.sibling).wait_recv()

    def left(self, key, place):
        self.copy(key, place, place, self.near.sibling).wait_send()

    def product(self, left, right):
        step = 256
        for side in (1, 0):
            start = self.base if side == 0 else self.other
            for i in range(self.half // step):
                rows = aligned(start + i * step, step)
                mixed = lax.dot_general(
                    left[:, rows],
                    right[...],
                    (((0,), (0,)), ((), ())),
                    preferred_element_type=jnp.float32,
                )
                self.partial[rows, :] = mixed.astype(jnp.bfloat16)
                if side == 1:
                    block = pl.ds(i * step, step)
                    self.copy(
                        ("pair", i), self.partial.at[rows], self.pair.at[block], self.near.sibling
                    ).start()

    def place(self, axis, k=0):
        return self.near.places[axis][k]

    def pair_sum(self):
        step = 256
        for i in range(self.half // step):
            block = pl.ds(i * step, step)
            self.arrived(("pair", i), self.pair.at[block])
            own = self.partial[aligned(self.base + i * step, step), :].astype(jnp.float32)
            total = own + self.pair[block, :].astype(jnp.float32)
            self.first[block, :] = total.astype(jnp.bfloat16)
        for k in (2, 1, 3):
            for part, (start, width, axis) in enumerate(self.parts):
                cols = pl.ds(start, width)
                self.copy(
                    ("first", part),
                    self.first.at[aligned(self.place(axis, k) * self.size, self.size), cols],
                    self.first_in.at[k - 1, :, cols],
                    self.near.step(**{axis: k}),
                ).start()

    def piece(self, part, steps, base=0):
        start, width, axis = self.parts[part]
        one, two = [name for name in "xyz" if name != axis]
        first, second = self.place(one, steps.get(one, 0)), self.place(two, steps.get(two, 0))
        row = (first * 2 + (second >> 1)) * 16 + base
        col = (second & 1) * (width // 2) + start
        return (aligned(row, 16), pl.ds(pl.multiple_of(col, LANES), width // 2))

    def landing(self, part):
        start, width, _ = self.parts[part]
        return pl.ds(start // 2, width // 2)

    def scatter_first(self):
        for part, (start, width, axis) in enumerate(self.parts):
            cols = pl.ds(start, width)
            self.arrived(("first", part), self.first_in.at[:, :, cols])
            total = self.first[aligned(self.place(axis) * self.size, self.size), cols].astype(jnp.float32)
            for k in range(3):
                total += self.first_in[k, :, cols].astype(jnp.float32)
            self.second[:, cols] = total.astype(jnp.bfloat16)
            for k, steps in enumerate(rest(axis)):
                self.copy(
                    ("second", part),
                    self.second.at[self.piece(part, steps)],
                    self.second_in.at[k, :, self.landing(part)],
                    self.near.step(**steps),
                ).start()

    def own_rows(self, part, k=0):
        return self.base + self.place(self.parts[part][2], k) * self.size

    def scatter_second(self):
        for part, (start, width, axis) in enumerate(self.parts):
            cols = self.landing(part)
            self.arrived(("second", part), self.second_in.at[:, :, cols])
            total = self.second[self.piece(part, {})].astype(jnp.float32)
            for k in range(15):
                total += self.second_in[k, :, cols].astype(jnp.float32)
            slices = self.piece(part, {}, self.own_rows(part))
            self.full[slices] = total.astype(jnp.bfloat16)
            place = self.full.at[slices]
            for steps in rest(axis):
                self.copy(("back", part), place, place, self.near.step(**steps)).start()

    def gather_second(self):
        for part, (start, width, axis) in enumerate(self.parts):
            cols = pl.ds(start, width)
            self.arrived(("back", part), self.second_in.at[:, :, self.landing(part)])
            place = self.full.at[aligned(self.own_rows(part), self.size), cols]
            for k in (2, 1, 3):
                self.copy(("last", part, 4 - k), place, place, self.near.step(**{axis: k})).start()
            self.copy(("across", part, 0), place, place, self.near.sibling).start()

    def gather_first(self):
        for k in (1, 3, 2):
            for part, (start, width, axis) in enumerate(self.parts):
                place = self.full.at[aligned(self.own_rows(part, k), self.size), pl.ds(start, width)]
                self.arrived(("last", part, k), place)
                self.copy(("across", part, k), place, place, self.near.sibling).start()

    def finish(self):
        turn = self.other - self.base
        for part, (start, width, axis) in enumerate(self.parts):
            cols = pl.ds(start, width)
            for k in range(4):
                rows = aligned(self.own_rows(part, k) + turn, self.size)
                self.arrived(("across", part, k), self.full.at[rows, cols])
        for part, (start, width, axis) in enumerate(self.parts):
            cols = pl.ds(start, width)
            self.left(("first", part), self.first_in.at[:, :, cols])
            self.left(("second", part), self.second_in.at[:, :, self.landing(part)])
            self.left(("back", part), self.second_in.at[:, :, self.landing(part)])
            block = self.full.at[pl.ds(0, self.size), cols]
            for k in (1, 2, 3):
                self.left(("last", part, k), block)
            for k in range(4):
                self.left(("across", part, k), block)
        for i in range(self.half // 256):
            self.left(("pair", i), self.pair.at[pl.ds(i * 256, 256)])


def reduction_scratch(parts, width):
    half = width // 2
    kind = jnp.bfloat16
    slots = 2 + 10 * len(parts)
    return [
        pltpu.VMEM((width, width), kind),
        pltpu.VMEM((half, width), kind),
        pltpu.VMEM((half, width), kind),
        pltpu.VMEM((3, half // 4, width), kind),
        pltpu.VMEM((half // 4, width), kind),
        pltpu.VMEM((15, half // 32, width // 2), kind),
        pltpu.SemaphoreType.DMA((slots,)),
        pltpu.SemaphoreType.DMA((slots,)),
    ]


def layer_kernel(
    n,
    document,
    summary,
    encoder_gain,
    memory_gain,
    summary_gain,
    query_weight,
    key_weight,
    value_weight,
    output_weight,
    cross_query,
    cross_key,
    cross_value,
    cross_output,
    encoder_cotangent,
    decoder_cotangent,
    encoded,
    decoded,
    own_full,
    cross_full,
    doc,
    states,
    weights,
    own_cotangent,
    cross_cotangent,
    normed,
    qkv_send,
    qkv_recv,
    sq_send,
    sq_recv,
    head_send,
    head_recv,
    kv_send,
    kv_recv,
    cross_send,
    cross_recv,
    value_low,
    value_high,
    load_sem,
    send_sem,
    recv_sem,
    *grad_refs,
):
    dp = lax.axis_index("dp")
    me = lax.axis_index("ctx")
    rows = doc.shape[0]
    count = states.shape[0]
    width = doc.shape[1]
    blocks = width // (2 * LANES)

    loads = [
        pltpu.make_async_copy(src, dst, load_sem.at[i])
        for i, (src, dst) in enumerate(
            [
                (document, doc),
                (query_weight, weights.at[0]),
                (key_weight, weights.at[1]),
                (value_weight, weights.at[2]),
                (summary, states),
                (cross_query, weights.at[4]),
                (output_weight, weights.at[3]),
                (cross_key, weights.at[5]),
                (cross_value, weights.at[6]),
                (encoder_cotangent, own_cotangent),
                (cross_output, weights.at[7]),
                (decoder_cotangent, cross_cotangent),
            ]
        )
    ]
    for i in (0, 2, 3):
        loads[i].start()

    near = Neighbours(dp, me)
    barrier = pltpu.get_barrier_semaphore()

    @pl.loop(1, n)
    def _(i):
        peer = lax.rem(me + i, n)
        pl.semaphore_signal(barrier, inc=1, device_id=(dp, peer), device_id_type=MESH)

    others = near.distant()
    for device in others:
        pl.semaphore_signal(barrier, inc=1, device_id=device, device_id_type=MESH)

    def remote(phase, peer, source, src, dst):
        return pltpu.make_async_remote_copy(
            src_ref=src,
            dst_ref=dst,
            send_sem=send_sem.at[phase, peer],
            recv_sem=recv_sem.at[phase, source],
            device_id=(dp, peer),
            device_id_type=MESH,
        )

    def local(phase, src, dst):
        return pltpu.make_async_copy(src, dst, recv_sem.at[phase, me])

    def start(phase, peer, src, dst):
        @pl.when(peer != me)
        def _():
            remote(phase, peer, me, src, dst).start()

        @pl.when(peer == me)
        def _():
            local(phase, src, dst).start()

    def wait_one(phase, source, src, dst):
        @pl.when(source != me)
        def _():
            remote(phase, source, source, src, dst).wait_recv()

        @pl.when(source == me)
        def _():
            local(phase, src, dst).wait()

    def wait_all(phase, src_of, dst_of):
        @pl.loop(0, n)
        def _(source):
            wait_one(phase, source, src_of(source), dst_of(source))

    def wait_sent(phase, src_of, dst_of):
        @pl.loop(0, n)
        def _(peer):
            @pl.when(peer != me)
            def _():
                remote(phase, peer, me, src_of(peer), dst_of(peer)).wait_send()

    def column(index):
        return pl.ds(pl.multiple_of(index * LANES, LANES), LANES)

    def wide(index):
        return pl.ds(pl.multiple_of(index * 2 * LANES, 2 * LANES), 2 * LANES)

    loads[0].wait()
    normed[...] = norm_rows(doc[...], encoder_gain[...])
    pl.semaphore_wait(barrier, n - 1 + len(others))
    loads[2].wait()
    loads[3].wait()
    for i in (1, 4, 5, 6, 7, 8, 9, 10, 11):
        loads[i].start()

    @pl.loop(0, blocks)
    def _(i):
        block = lax.rem(lax.div(me, 2) + (blocks - 1) - i, blocks)
        for t in (1, 2):
            part = matmul(normed[...], weights[t, :, wide(block)]).astype(jnp.bfloat16)
            qkv_send[2 * block, t] = part[:, :LANES]
            qkv_send[2 * block + 1, t] = part[:, LANES:]
        for half in range(2):
            peer = 2 * block + half
            start(SELF_KV, peer, qkv_send.at[peer, pl.ds(1, 2)], qkv_recv.at[pl.ds(1, 2), me])

    loads[1].wait()

    @pl.loop(0, blocks)
    def _(i):
        part = matmul(normed[...], weights[0, :, wide(i)]).astype(jnp.bfloat16)
        qkv_send[2 * i, 0] = part[:, :LANES]
        qkv_send[2 * i + 1, 0] = part[:, LANES:]

    loads[4].wait()
    loads[5].wait()
    normed[0:count, :] = norm_rows(states[...], summary_gain[...])

    @pl.loop(0, blocks)
    def _(i):
        part = matmul(normed[0:count, :], weights[4, :, wide(i)]).astype(jnp.bfloat16)
        sq_send[2 * i] = part[:, :LANES]
        sq_send[2 * i + 1] = part[:, LANES:]

    kv_sent = lambda p: qkv_send.at[p, pl.ds(1, 2)], lambda p: qkv_recv.at[pl.ds(1, 2), me]
    wait_sent(SELF_KV, *kv_sent)

    @pl.loop(0, n)
    def _(i):
        peer = lax.rem(me + n - i, n)
        start(SELF_Q, peer, qkv_send.at[peer, 0], qkv_recv.at[0, me])

    lane = lax.broadcasted_iota(jnp.int32, (1, LANES), 1)
    low = lane < HEAD_DIM
    zero = jnp.zeros((), jnp.bfloat16)
    one = jnp.ones((), jnp.bfloat16)

    def set_values(ref):
        values = ref[...].reshape(n * rows, LANES)
        value_low[...] = jnp.where(low, values, one)
        value_high[...] = jnp.where(low, one, values)

    def attend(query, keys):
        def head(part, values):
            scores = lax.dot_general(
                part, keys, (((1,), (1,)), ((), ())), preferred_element_type=jnp.float32
            )
            top = jnp.max(scores, axis=-1, keepdims=True)
            weight = jnp.exp(scores - top).astype(jnp.bfloat16)
            return matmul(weight, values[...])

        left = head(jnp.where(low, query, zero), value_low)
        right = head(jnp.where(low, zero, query), value_high)
        mixed = jnp.where(low, left, right)
        total = jnp.where(
            low, pltpu.roll(left, HEAD_DIM, 1), pltpu.roll(right, HEAD_DIM, 1)
        )
        return (mixed / total).astype(jnp.bfloat16)

    wait_all(
        SELF_KV, lambda s: qkv_send.at[s, pl.ds(1, 2)], lambda s: qkv_recv.at[pl.ds(1, 2), s]
    )
    set_values(qkv_recv.at[2])

    @pl.loop(0, n)
    def _(i):
        peer = lax.rem(me + i, n)
        wait_one(SELF_Q, peer, qkv_send.at[peer, 0], qkv_recv.at[0, peer])
        keys = qkv_recv[1].reshape(n * rows, LANES)
        head_send[peer] = attend(qkv_recv[0, peer], keys)
        start(HEAD, peer, head_send.at[peer], head_recv.at[:, column(me)])

        @pl.when(i == 2)
        def _():
            @pl.loop(0, n)
            def _(p):
                start(SQ, p, sq_send.at[p], sq_recv.at[me])

    loads[6].wait()
    wait_all(HEAD, lambda s: head_send.at[s], lambda s: head_recv.at[:, column(s)])

    @pl.loop(0, blocks)
    def _(i):
        mixed = matmul(head_recv[...], weights[3, :, wide(i)])
        encoded[:, wide(i)] = (doc[:, wide(i)].astype(jnp.float32) + mixed).astype(jnp.bfloat16)

    own_refs = Reduction(near, OWN_PARTS, own_full, *grad_refs[:REFS])
    cross_refs = Reduction(near, CROSS_PARTS, cross_full, *grad_refs[REFS:])

    normed[...] = norm_rows(encoded[...], memory_gain[...])
    loads[7].wait()
    loads[8].wait()

    @pl.loop(0, blocks)
    def _(i):
        block = lax.rem(lax.div(me, 2) + (blocks - 1) - i, blocks)
        for t in range(2):
            part = matmul(normed[...], weights[5 + t, :, wide(block)]).astype(jnp.bfloat16)
            kv_send[2 * block, t] = part[:, :LANES]
            kv_send[2 * block + 1, t] = part[:, LANES:]
        for half in range(2):
            peer = 2 * block + half
            start(KV, peer, kv_send.at[peer], kv_recv.at[:, me])

    loads[9].wait()
    own_refs.product(head_recv, own_cotangent)
    own_refs.pair_sum()

    wait_all(SQ, lambda s: sq_send.at[s], lambda s: sq_recv.at[s])
    wait_all(KV, lambda s: kv_send.at[s], lambda s: kv_recv.at[:, s])
    set_values(kv_recv.at[1])

    def cross_block(i):
        pair = lax.rem(lax.div(me, 2) + 1 + i, n // 2)
        keys = kv_recv[0].reshape(n * rows, LANES)
        query = sq_recv[pl.ds(2 * pair, 2)].reshape(2 * count, LANES)
        mixed = attend(query, keys)
        cross_send[2 * pair] = mixed[:count]
        cross_send[2 * pair + 1] = mixed[count:]
        for half in range(2):
            peer = 2 * pair + half
            start(CROSS, peer, cross_send.at[peer], cross_recv.at[:, column(me)])

    pl.loop(0, n // 2 - 1)(cross_block)
    own_refs.scatter_first()
    cross_block(n // 2 - 1)
    loads[11].wait()
    wait_all(CROSS, lambda s: cross_send.at[s], lambda s: cross_recv.at[:, column(s)])
    cross_refs.product(cross_recv, cross_cotangent)
    own_refs.scatter_second()
    cross_refs.pair_sum()
    loads[10].wait()

    @pl.loop(0, blocks)
    def _(i):
        mixed = matmul(cross_recv[...], weights[7, :, wide(i)])
        decoded[:, wide(i)] = (states[:, wide(i)].astype(jnp.float32) + mixed).astype(jnp.bfloat16)

    own_refs.gather_second()
    cross_refs.scatter_first()
    cross_refs.scatter_second()
    own_refs.gather_first()
    cross_refs.gather_second()
    cross_refs.gather_first()
    own_refs.finish()
    cross_refs.finish()
    wait_sent(SELF_Q, lambda p: qkv_send.at[p, 0], lambda p: qkv_recv.at[0, me])
    wait_sent(SQ, lambda p: sq_send.at[p], lambda p: sq_recv.at[me])
    wait_sent(HEAD, lambda p: head_send.at[p], lambda p: head_recv.at[:, column(me)])
    wait_sent(KV, lambda p: kv_send.at[p], lambda p: kv_recv.at[:, me])
    wait_sent(CROSS, lambda p: cross_send.at[p], lambda p: cross_recv.at[:, column(me)])


def solution(mesh):
    n = mesh.shape["ctx"]

    def body(
        document,
        summary,
        encoder_gain,
        query_weight,
        key_weight,
        value_weight,
        output_weight,
        memory_gain,
        summary_gain,
        cross_query,
        cross_key,
        cross_value,
        cross_output,
        encoder_cotangent,
        decoder_cotangent,
    ):
        rows, width = document.shape[1:]
        count = summary.shape[1]
        half = jnp.bfloat16
        hbm = pl.BlockSpec(memory_space=pl.ANY)
        vmem = pl.BlockSpec(memory_space=pltpu.VMEM)
        shapes = [(rows, width), (count, width), (width, width), (width, width)]
        encoded, decoded, own_grad, cross_grad = pl.pallas_call(
            functools.partial(layer_kernel, n),
            out_shape=[pltpu.VMEM(shape, half) for shape in shapes],
            in_specs=[hbm] * 2 + [vmem] * 3 + [hbm] * 10,
            out_specs=[vmem] * 4,
            scratch_shapes=[
                pltpu.VMEM((rows, width), half),
                pltpu.VMEM((count, width), half),
                pltpu.VMEM((8, width, width), half),
                pltpu.VMEM((rows, width), half),
                pltpu.VMEM((count, width), half),
                pltpu.VMEM((rows, width), half),
                pltpu.VMEM((n, 3, rows, LANES), half),
                pltpu.VMEM((3, n, rows, LANES), half),
                pltpu.VMEM((n, count, LANES), half),
                pltpu.VMEM((n, count, LANES), half),
                pltpu.VMEM((n, rows, LANES), half),
                pltpu.VMEM((rows, width), half),
                pltpu.VMEM((n, 2, rows, LANES), half),
                pltpu.VMEM((2, n, rows, LANES), half),
                pltpu.VMEM((n, count, LANES), half),
                pltpu.VMEM((count, width), half),
                pltpu.VMEM((n * rows, LANES), half),
                pltpu.VMEM((n * rows, LANES), half),
                pltpu.SemaphoreType.DMA((12,)),
                pltpu.SemaphoreType.DMA((6, n)),
                pltpu.SemaphoreType.DMA((6, n)),
                *reduction_scratch(OWN_PARTS, width),
                *reduction_scratch(CROSS_PARTS, width),
            ],
            compiler_params=pltpu.CompilerParams(
                collective_id=0, has_side_effects=True, vmem_limit_bytes=50 * 2**20
            ),
        )(
            document[0],
            summary[0],
            encoder_gain[None],
            memory_gain[None],
            summary_gain[None],
            query_weight,
            key_weight,
            value_weight,
            output_weight,
            cross_query,
            cross_key,
            cross_value,
            cross_output,
            encoder_cotangent[0],
            decoder_cotangent[0],
        )
        return (
            encoded[None],
            decoded[None],
            own_grad,
            cross_grad,
        )

    rows_spec = P("dp", "ctx", None)
    return jax.shard_map(
        body,
        mesh=mesh,
        in_specs=(rows_spec, rows_spec) + (P(),) * 11 + (rows_spec, rows_spec),
        out_specs=(rows_spec, rows_spec, P(), P()),
        check_vma=False,
    )
```

```python
import functools

import jax
import jax.numpy as jnp
from jax import lax
from jax.experimental import pallas as pl
from jax.experimental.pallas import tpu as pltpu
from jax.sharding import PartitionSpec as P

HEADS = 16
HEAD_DIM = 64
LANES = 128
MESH = pl.DeviceIdType.MESH
SELF_KV, SELF_Q, SQ, HEAD, KV, KV_LATE, CROSS = range(7)


def norm_rows(rows, gain):
    values = rows.astype(jnp.float32)
    scale = lax.rsqrt(jnp.mean(values * values, axis=-1, keepdims=True) + 1e-06)
    return (values * scale * gain).astype(jnp.bfloat16)


def matmul(left, right):
    return jnp.dot(left, right, preferred_element_type=jnp.float32)


OWN_PARTS = ((0, 512, "x"), (512, 256, "y"), (768, 256, "z"))
CROSS_PARTS = ((0, 512, "y"), (512, 256, "z"), (768, 256, "x"))
REFS = 8


class Neighbours:
    def __init__(self, dp, ctx):
        self.core = dp & 1
        low, high = (dp >> 1) & 1, ctx >> 2
        place = {"x": dp >> 2, "y": ctx & 3, "z": high * 2 + low}
        self.places = {axis: [(start + k) & 3 for k in range(4)] for axis, start in place.items()}
        self.dp_x = [x * 4 for x in self.places["x"]]
        self.dp_z = [(z & 1) * 2 + self.core for z in self.places["z"]]
        self.ctx_z = [(z >> 1) * 4 for z in self.places["z"]]
        self.sibling = (dp + 1 - 2 * self.core, ctx)

    def step(self, x=0, y=0, z=0):
        return (self.dp_x[x] + self.dp_z[z], self.ctx_z[z] + self.places["y"][y])

    def distant(self):
        parts = OWN_PARTS + CROSS_PARTS
        reached = {tuple(k if axis == name else 0 for name in "xyz") for *_, axis in parts for k in (1, 2, 3)}
        for *_, axis in parts:
            for steps in rest(axis):
                reached.add(tuple(steps.get(name, 0) for name in "xyz"))
        reached = sorted((i, j, k) for i, j, k in reached if i > 0 or k % 2 == 1)
        return [self.sibling] + [self.step(*steps) for steps in reached]


def rest(axis):
    one, two = [name for name in "xyz" if name != axis]
    return [{one: i, two: j} for i in range(4) for j in range(4) if i or j]


def aligned(start, size):
    return pl.ds(pl.multiple_of(start, size), size)


class Reduction:
    def __init__(
        self, near, parts, full, partial, pair, first, first_in, second, second_in, send, recv
    ):
        self.near = near
        self.parts = parts
        self.partial, self.pair, self.full = partial, pair, full
        self.first, self.first_in = first, first_in
        self.second, self.second_in = second, second_in
        self.send, self.recv = send, recv
        self.half = pair.shape[0]
        self.size = self.half // 4
        self.base = near.core * self.half
        self.other = self.half - self.base
        self.slots = {}

    def copy(self, key, src, dst, device):
        slot = self.slots.setdefault(key, len(self.slots))
        return pltpu.make_async_remote_copy(
            src_ref=src,
            dst_ref=dst,
            send_sem=self.send.at[slot],
            recv_sem=self.recv.at[slot],
            device_id=device,
            device_id_type=MESH,
        )

    def arrived(self, key, place):
        self.copy(key, place, place, self.near.sibling).wait_recv()

    def left(self, key, place):
        self.copy(key, place, place, self.near.sibling).wait_send()

    def product(self, left, right):
        step = 256
        for side in (1, 0):
            start = self.base if side == 0 else self.other
            for i in range(self.half // step):
                rows = aligned(start + i * step, step)
                mixed = lax.dot_general(
                    left[:, rows],
                    right[...],
                    (((0,), (0,)), ((), ())),
                    preferred_element_type=jnp.float32,
                )
                self.partial[rows, :] = mixed.astype(jnp.bfloat16)
                if side == 1:
                    block = pl.ds(i * step, step)
                    self.copy(
                        ("pair", i), self.partial.at[rows], self.pair.at[block], self.near.sibling
                    ).start()

    def place(self, axis, k=0):
        return self.near.places[axis][k]

    def pair_sum(self):
        step = 256
        for i in range(self.half // step):
            block = pl.ds(i * step, step)
            self.arrived(("pair", i), self.pair.at[block])
            own = self.partial[aligned(self.base + i * step, step), :].astype(jnp.float32)
            total = own + self.pair[block, :].astype(jnp.float32)
            self.first[block, :] = total.astype(jnp.bfloat16)
        for k in (2, 1, 3):
            for part, (start, width, axis) in enumerate(self.parts):
                cols = pl.ds(start, width)
                self.copy(
                    ("first", part),
                    self.first.at[aligned(self.place(axis, k) * self.size, self.size), cols],
                    self.first_in.at[k - 1, :, cols],
                    self.near.step(**{axis: k}),
                ).start()

    def piece(self, part, steps, base=0):
        start, width, axis = self.parts[part]
        one, two = [name for name in "xyz" if name != axis]
        first, second = self.place(one, steps.get(one, 0)), self.place(two, steps.get(two, 0))
        row = (first * 2 + (second >> 1)) * 16 + base
        col = (second & 1) * (width // 2) + start
        return (aligned(row, 16), pl.ds(pl.multiple_of(col, LANES), width // 2))

    def landing(self, part):
        start, width, _ = self.parts[part]
        return pl.ds(start // 2, width // 2)

    def scatter_first(self):
        for part, (start, width, axis) in enumerate(self.parts):
            cols = pl.ds(start, width)
            self.arrived(("first", part), self.first_in.at[:, :, cols])
            total = self.first[aligned(self.place(axis) * self.size, self.size), cols].astype(jnp.float32)
            for k in range(3):
                total += self.first_in[k, :, cols].astype(jnp.float32)
            self.second[:, cols] = total.astype(jnp.bfloat16)
            for k, steps in enumerate(rest(axis)):
                self.copy(
                    ("second", part),
                    self.second.at[self.piece(part, steps)],
                    self.second_in.at[k, :, self.landing(part)],
                    self.near.step(**steps),
                ).start()

    def own_rows(self, part, k=0):
        return self.base + self.place(self.parts[part][2], k) * self.size

    def scatter_second(self):
        for part, (start, width, axis) in enumerate(self.parts):
            cols = self.landing(part)
            self.arrived(("second", part), self.second_in.at[:, :, cols])
            total = self.second[self.piece(part, {})].astype(jnp.float32)
            for k in range(15):
                total += self.second_in[k, :, cols].astype(jnp.float32)
            slices = self.piece(part, {}, self.own_rows(part))
            self.full[slices] = total.astype(jnp.bfloat16)
            place = self.full.at[slices]
            for steps in rest(axis):
                self.copy(("back", part), place, place, self.near.step(**steps)).start()

    def gather_second(self):
        for part, (start, width, axis) in enumerate(self.parts):
            cols = pl.ds(start, width)
            self.arrived(("back", part), self.second_in.at[:, :, self.landing(part)])
            place = self.full.at[aligned(self.own_rows(part), self.size), cols]
            for k in (2, 1, 3):
                self.copy(("last", part, 4 - k), place, place, self.near.step(**{axis: k})).start()
            self.copy(("across", part, 0), place, place, self.near.sibling).start()

    def gather_first(self):
        for k in (1, 3, 2):
            for part, (start, width, axis) in enumerate(self.parts):
                place = self.full.at[aligned(self.own_rows(part, k), self.size), pl.ds(start, width)]
                self.arrived(("last", part, k), place)
                self.copy(("across", part, k), place, place, self.near.sibling).start()

    def finish(self):
        turn = self.other - self.base
        for part, (start, width, axis) in enumerate(self.parts):
            cols = pl.ds(start, width)
            for k in range(4):
                rows = aligned(self.own_rows(part, k) + turn, self.size)
                self.arrived(("across", part, k), self.full.at[rows, cols])
        for part, (start, width, axis) in enumerate(self.parts):
            cols = pl.ds(start, width)
            self.left(("first", part), self.first_in.at[:, :, cols])
            self.left(("second", part), self.second_in.at[:, :, self.landing(part)])
            self.left(("back", part), self.second_in.at[:, :, self.landing(part)])
            block = self.full.at[pl.ds(0, self.size), cols]
            for k in (1, 2, 3):
                self.left(("last", part, k), block)
            for k in range(4):
                self.left(("across", part, k), block)
        for i in range(self.half // 256):
            self.left(("pair", i), self.pair.at[pl.ds(i * 256, 256)])


def reduction_scratch(parts, width):
    half = width // 2
    kind = jnp.bfloat16
    slots = 2 + 10 * len(parts)
    return [
        pltpu.VMEM((width, width), kind),
        pltpu.VMEM((half, width), kind),
        pltpu.VMEM((half, width), kind),
        pltpu.VMEM((3, half // 4, width), kind),
        pltpu.VMEM((half // 4, width), kind),
        pltpu.VMEM((15, half // 32, width // 2), kind),
        pltpu.SemaphoreType.DMA((slots,)),
        pltpu.SemaphoreType.DMA((slots,)),
    ]


def layer_kernel(
    n,
    document,
    summary,
    encoder_gain,
    memory_gain,
    summary_gain,
    query_weight,
    key_weight,
    value_weight,
    output_weight,
    cross_query,
    cross_key,
    cross_value,
    cross_output,
    encoder_cotangent,
    decoder_cotangent,
    encoded,
    decoded,
    own_full,
    cross_full,
    doc,
    states,
    weights,
    own_cotangent,
    cross_cotangent,
    normed,
    qkv_send,
    qkv_recv,
    sq_send,
    sq_recv,
    head_send,
    head_recv,
    kv_send,
    kv_recv,
    early,
    cross_send,
    cross_recv,
    value_low,
    value_high,
    load_sem,
    send_sem,
    recv_sem,
    *grad_refs,
):
    dp = lax.axis_index("dp")
    me = lax.axis_index("ctx")
    rows = doc.shape[0]
    count = states.shape[0]
    width = doc.shape[1]
    blocks = width // (2 * LANES)

    loads = [
        pltpu.make_async_copy(src, dst, load_sem.at[i])
        for i, (src, dst) in enumerate(
            [
                (document, doc),
                (query_weight, weights.at[0]),
                (key_weight, weights.at[1]),
                (value_weight, weights.at[2]),
                (summary, states),
                (cross_query, weights.at[4]),
                (output_weight, weights.at[3]),
                (cross_key, weights.at[5]),
                (cross_value, weights.at[6]),
                (encoder_cotangent, own_cotangent),
                (cross_output, weights.at[7]),
                (decoder_cotangent, cross_cotangent),
            ]
        )
    ]
    for i in (0, 2, 3):
        loads[i].start()

    near = Neighbours(dp, me)
    barrier = pltpu.get_barrier_semaphore()

    @pl.loop(1, n)
    def _(i):
        peer = lax.rem(me + i, n)
        pl.semaphore_signal(barrier, inc=1, device_id=(dp, peer), device_id_type=MESH)

    others = near.distant()
    for device in others:
        pl.semaphore_signal(barrier, inc=1, device_id=device, device_id_type=MESH)

    def remote(phase, peer, source, src, dst):
        return pltpu.make_async_remote_copy(
            src_ref=src,
            dst_ref=dst,
            send_sem=send_sem.at[phase, peer],
            recv_sem=recv_sem.at[phase, source],
            device_id=(dp, peer),
            device_id_type=MESH,
        )

    def local(phase, src, dst):
        return pltpu.make_async_copy(src, dst, recv_sem.at[phase, me])

    def start(phase, peer, src, dst):
        @pl.when(peer != me)
        def _():
            remote(phase, peer, me, src, dst).start()

        @pl.when(peer == me)
        def _():
            local(phase, src, dst).start()

    def wait_one(phase, source, src, dst):
        @pl.when(source != me)
        def _():
            remote(phase, source, source, src, dst).wait_recv()

        @pl.when(source == me)
        def _():
            local(phase, src, dst).wait()

    def wait_all(phase, src_of, dst_of):
        @pl.loop(0, n)
        def _(source):
            wait_one(phase, source, src_of(source), dst_of(source))

    def wait_sent(phase, src_of, dst_of):
        @pl.loop(0, n)
        def _(peer):
            @pl.when(peer != me)
            def _():
                remote(phase, peer, me, src_of(peer), dst_of(peer)).wait_send()

    def column(index):
        return pl.ds(pl.multiple_of(index * LANES, LANES), LANES)

    def wide(index):
        return pl.ds(pl.multiple_of(index * 2 * LANES, 2 * LANES), 2 * LANES)

    loads[0].wait()
    normed[...] = norm_rows(doc[...], encoder_gain[...])
    pl.semaphore_wait(barrier, n - 1 + len(others))
    loads[2].wait()
    loads[3].wait()
    for i in (1, 4, 5, 6, 7, 8, 9, 10, 11):
        loads[i].start()

    @pl.loop(0, blocks)
    def _(i):
        block = lax.rem(lax.div(me, 2) + (blocks - 1) - i, blocks)
        for t in (1, 2):
            part = matmul(normed[...], weights[t, :, wide(block)]).astype(jnp.bfloat16)
            qkv_send[2 * block, t] = part[:, :LANES]
            qkv_send[2 * block + 1, t] = part[:, LANES:]
        for half in range(2):
            peer = 2 * block + half
            start(SELF_KV, peer, qkv_send.at[peer, pl.ds(1, 2)], qkv_recv.at[pl.ds(1, 2), me])

    loads[1].wait()

    @pl.loop(0, blocks)
    def _(i):
        part = matmul(normed[...], weights[0, :, wide(i)]).astype(jnp.bfloat16)
        qkv_send[2 * i, 0] = part[:, :LANES]
        qkv_send[2 * i + 1, 0] = part[:, LANES:]

    loads[4].wait()
    loads[5].wait()
    normed[0:count, :] = norm_rows(states[...], summary_gain[...])

    @pl.loop(0, blocks)
    def _(i):
        part = matmul(normed[0:count, :], weights[4, :, wide(i)]).astype(jnp.bfloat16)
        sq_send[2 * i] = part[:, :LANES]
        sq_send[2 * i + 1] = part[:, LANES:]

    kv_sent = lambda p: qkv_send.at[p, pl.ds(1, 2)], lambda p: qkv_recv.at[pl.ds(1, 2), me]
    wait_sent(SELF_KV, *kv_sent)

    @pl.loop(0, n)
    def _(i):
        peer = lax.rem(me + n - i, n)
        start(SELF_Q, peer, qkv_send.at[peer, 0], qkv_recv.at[0, me])

    lane = lax.broadcasted_iota(jnp.int32, (1, LANES), 1)
    low = lane < HEAD_DIM
    zero = jnp.zeros((), jnp.bfloat16)
    one = jnp.ones((), jnp.bfloat16)

    def set_values(ref):
        values = ref[...].reshape(n * rows, LANES)
        value_low[...] = jnp.where(low, values, one)
        value_high[...] = jnp.where(low, one, values)

    def attend_part(query, keys, places):
        def head(part, values):
            scores = lax.dot_general(
                part, keys, (((1,), (1,)), ((), ())), preferred_element_type=jnp.float32
            )
            top = jnp.max(scores, axis=-1, keepdims=True)
            weight = jnp.exp(scores - top).astype(jnp.bfloat16)
            return matmul(weight, values[places, :]), top

        left, left_top = head(jnp.where(low, query, zero), value_low)
        right, right_top = head(jnp.where(low, zero, query), value_high)
        mixed = jnp.where(low, left, right)
        total = jnp.where(
            low, pltpu.roll(left, HEAD_DIM, 1), pltpu.roll(right, HEAD_DIM, 1)
        )
        return mixed, total, jnp.where(low, left_top, right_top)

    def attend(query, keys):
        mixed, total, _ = attend_part(query, keys, pl.ds(0, n * rows))
        return (mixed / total).astype(jnp.bfloat16)

    wait_all(
        SELF_KV, lambda s: qkv_send.at[s, pl.ds(1, 2)], lambda s: qkv_recv.at[pl.ds(1, 2), s]
    )
    set_values(qkv_recv.at[2])

    @pl.loop(0, n)
    def _(i):
        peer = lax.rem(me + i, n)
        wait_one(SELF_Q, peer, qkv_send.at[peer, 0], qkv_recv.at[0, peer])
        keys = qkv_recv[1].reshape(n * rows, LANES)
        head_send[peer] = attend(qkv_recv[0, peer], keys)
        start(HEAD, peer, head_send.at[peer], head_recv.at[:, column(me)])

        @pl.when(i == 2)
        def _():
            @pl.loop(0, n)
            def _(p):
                start(SQ, p, sq_send.at[p], sq_recv.at[me])

    loads[6].wait()
    wait_all(HEAD, lambda s: head_send.at[s], lambda s: head_recv.at[:, column(s)])

    own_refs = Reduction(near, OWN_PARTS, own_full, *grad_refs[:REFS])
    cross_refs = Reduction(near, CROSS_PARTS, cross_full, *grad_refs[REFS:])
    loads[7].wait()
    loads[8].wait()

    for side, phase in enumerate((KV, KV_LATE)):
        place = pl.ds(side * (rows // 2), rows // 2)

        @pl.loop(0, blocks)
        def _(i):
            mixed = matmul(head_recv[place, :], weights[3, :, wide(i)])
            total = doc[place, wide(i)].astype(jnp.float32) + mixed
            encoded[place, wide(i)] = total.astype(jnp.bfloat16)

        normed[place, :] = norm_rows(encoded[place, :], memory_gain[...])

        @pl.loop(0, blocks)
        def _(i):
            block = lax.rem(lax.div(me, 2) + (blocks - 1) - i, blocks)
            for t in range(2):
                part = matmul(normed[place, :], weights[5 + t, :, wide(block)]).astype(jnp.bfloat16)
                kv_send[2 * block, side, t] = part[:, :LANES]
                kv_send[2 * block + 1, side, t] = part[:, LANES:]
            for half in range(2):
                peer = 2 * block + half
                start(phase, peer, kv_send.at[peer, side], kv_recv.at[side, :, me])

    loads[9].wait()
    own_refs.product(head_recv, own_cotangent)
    own_refs.pair_sum()

    wait_all(SQ, lambda s: sq_send.at[s], lambda s: sq_recv.at[s])
    span = n * rows // 2

    def ready(side, phase):
        wait_all(phase, lambda s: kv_send.at[s, side], lambda s: kv_recv.at[side, :, s])
        values = kv_recv[side, 1].reshape(span, LANES)
        value_low[pl.ds(side * span, span), :] = jnp.where(low, values, one)
        value_high[pl.ds(side * span, span), :] = jnp.where(low, one, values)

    def cross_part(pair, side):
        query = sq_recv[pl.ds(2 * pair, 2)].reshape(2 * count, LANES)
        keys = kv_recv[side, 0].reshape(span, LANES)
        return attend_part(query, keys, pl.ds(side * span, span))

    ready(0, KV)

    @pl.loop(0, n // 2)
    def _(pair):
        for t, value in enumerate(cross_part(pair, 0)):
            early[t, pair] = value

    ready(1, KV_LATE)

    def cross_block(i):
        pair = lax.rem(lax.div(me, 2) + 1 + i, n // 2)
        mixed, total, top = cross_part(pair, 1)
        best = jnp.maximum(top, early[2, pair])
        fade, late = jnp.exp(early[2, pair] - best), jnp.exp(top - best)
        mixed = mixed * late + early[0, pair] * fade
        total = total * late + early[1, pair] * fade
        mixed = (mixed / total).astype(jnp.bfloat16)
        cross_send[2 * pair] = mixed[:count]
        cross_send[2 * pair + 1] = mixed[count:]
        for half in range(2):
            peer = 2 * pair + half
            start(CROSS, peer, cross_send.at[peer], cross_recv.at[:, column(me)])

    pl.loop(0, n // 2 - 1)(cross_block)
    own_refs.scatter_first()
    cross_block(n // 2 - 1)
    loads[11].wait()
    wait_all(CROSS, lambda s: cross_send.at[s], lambda s: cross_recv.at[:, column(s)])
    cross_refs.product(cross_recv, cross_cotangent)
    own_refs.scatter_second()
    cross_refs.pair_sum()
    loads[10].wait()

    @pl.loop(0, blocks)
    def _(i):
        mixed = matmul(cross_recv[...], weights[7, :, wide(i)])
        decoded[:, wide(i)] = (states[:, wide(i)].astype(jnp.float32) + mixed).astype(jnp.bfloat16)

    own_refs.gather_second()
    cross_refs.scatter_first()
    cross_refs.scatter_second()
    own_refs.gather_first()
    cross_refs.gather_second()
    cross_refs.gather_first()
    own_refs.finish()
    cross_refs.finish()
    wait_sent(SELF_Q, lambda p: qkv_send.at[p, 0], lambda p: qkv_recv.at[0, me])
    wait_sent(SQ, lambda p: sq_send.at[p], lambda p: sq_recv.at[me])
    wait_sent(HEAD, lambda p: head_send.at[p], lambda p: head_recv.at[:, column(me)])
    for side, phase in enumerate((KV, KV_LATE)):
        wait_sent(phase, lambda p: kv_send.at[p, side], lambda p: kv_recv.at[side, :, me])
    wait_sent(CROSS, lambda p: cross_send.at[p], lambda p: cross_recv.at[:, column(me)])


def store_kernel(*refs):
    copies = [
        pltpu.make_async_copy(src, dst, refs[8].at[i])
        for i, (src, dst) in enumerate(zip(refs[:4], refs[4:8]))
    ]
    for copy in copies:
        copy.start()
    for copy in copies:
        copy.wait()


def solution(mesh):
    n = mesh.shape["ctx"]

    def body(
        document,
        summary,
        encoder_gain,
        query_weight,
        key_weight,
        value_weight,
        output_weight,
        memory_gain,
        summary_gain,
        cross_query,
        cross_key,
        cross_value,
        cross_output,
        encoder_cotangent,
        decoder_cotangent,
    ):
        rows, width = document.shape[1:]
        count = summary.shape[1]
        half = jnp.bfloat16
        hbm = pl.BlockSpec(memory_space=pl.ANY)
        vmem = pl.BlockSpec(memory_space=pltpu.VMEM)
        shapes = [(rows, width), (count, width), (width, width), (width, width)]
        results = pl.pallas_call(
            functools.partial(layer_kernel, n),
            out_shape=[pltpu.VMEM(shape, half) for shape in shapes],
            in_specs=[hbm] * 2 + [vmem] * 3 + [hbm] * 10,
            out_specs=[vmem] * 4,
            scratch_shapes=[
                pltpu.VMEM((rows, width), half),
                pltpu.VMEM((count, width), half),
                pltpu.VMEM((8, width, width), half),
                pltpu.VMEM((rows, width), half),
                pltpu.VMEM((count, width), half),
                pltpu.VMEM((rows, width), half),
                pltpu.VMEM((n, 3, rows, LANES), half),
                pltpu.VMEM((3, n, rows, LANES), half),
                pltpu.VMEM((n, count, LANES), half),
                pltpu.VMEM((n, count, LANES), half),
                pltpu.VMEM((n, rows, LANES), half),
                pltpu.VMEM((rows, width), half),
                pltpu.VMEM((n, 2, 2, rows // 2, LANES), half),
                pltpu.VMEM((2, 2, n, rows // 2, LANES), half),
                pltpu.VMEM((3, n // 2, 2 * count, LANES), jnp.float32),
                pltpu.VMEM((n, count, LANES), half),
                pltpu.VMEM((count, width), half),
                pltpu.VMEM((n * rows, LANES), half),
                pltpu.VMEM((n * rows, LANES), half),
                pltpu.SemaphoreType.DMA((12,)),
                pltpu.SemaphoreType.DMA((7, n)),
                pltpu.SemaphoreType.DMA((7, n)),
                *reduction_scratch(OWN_PARTS, width),
                *reduction_scratch(CROSS_PARTS, width),
            ],
            compiler_params=pltpu.CompilerParams(
                collective_id=0, has_side_effects=True, vmem_limit_bytes=50 * 2**20
            ),
        )(
            document[0],
            summary[0],
            encoder_gain[None],
            memory_gain[None],
            summary_gain[None],
            query_weight,
            key_weight,
            value_weight,
            output_weight,
            cross_query,
            cross_key,
            cross_value,
            cross_output,
            encoder_cotangent[0],
            decoder_cotangent[0],
        )
        encoded, decoded, own_grad, cross_grad = pl.pallas_call(
            store_kernel,
            out_shape=[jax.ShapeDtypeStruct(shape, half) for shape in shapes],
            in_specs=[vmem] * 4,
            out_specs=[hbm] * 4,
            scratch_shapes=[pltpu.SemaphoreType.DMA((4,))],
            compiler_params=pltpu.CompilerParams(vmem_limit_bytes=4 * 2**20),
        )(*[pltpu.with_memory_space_constraint(result, pltpu.VMEM) for result in results])
        return (
            encoded[None],
            decoded[None],
            own_grad,
            cross_grad,
        )

    rows_spec = P("dp", "ctx", None)
    return jax.shard_map(
        body,
        mesh=mesh,
        in_specs=(rows_spec, rows_spec) + (P(),) * 11 + (rows_spec, rows_spec),
        out_specs=(rows_spec, rows_spec, P(), P()),
        check_vma=False,
    )
```

```python
import functools

import jax
import jax.numpy as jnp
from jax import lax
from jax.experimental import pallas as pl
from jax.experimental.pallas import tpu as pltpu
from jax.sharding import PartitionSpec as P

HEADS = 16
HEAD_DIM = 64
LANES = 128
MESH = pl.DeviceIdType.MESH
SELF_KV, SELF_Q, SQ, HEAD, KV, KV_LATE, CROSS = range(7)


def norm_rows(rows, gain):
    values = rows.astype(jnp.float32)
    scale = lax.rsqrt(jnp.mean(values * values, axis=-1, keepdims=True) + 1e-06)
    return (values * scale * gain).astype(jnp.bfloat16)


def matmul(left, right):
    return jnp.dot(left, right, preferred_element_type=jnp.float32)


OWN_PARTS = ((0, 512, "x"), (512, 256, "y"), (768, 256, "z"))
CROSS_PARTS = ((0, 512, "y"), (512, 256, "z"), (768, 256, "x"))
REFS = 8


class Neighbours:
    def __init__(self, dp, ctx):
        self.core = dp & 1
        low, high = (dp >> 1) & 1, ctx >> 2
        place = {"x": dp >> 2, "y": ctx & 3, "z": high * 2 + low}
        self.places = {axis: [(start + k) & 3 for k in range(4)] for axis, start in place.items()}
        self.dp_x = [x * 4 for x in self.places["x"]]
        self.dp_z = [(z & 1) * 2 + self.core for z in self.places["z"]]
        self.ctx_z = [(z >> 1) * 4 for z in self.places["z"]]
        self.sibling = (dp + 1 - 2 * self.core, ctx)

    def step(self, x=0, y=0, z=0):
        return (self.dp_x[x] + self.dp_z[z], self.ctx_z[z] + self.places["y"][y])

    def distant(self):
        parts = OWN_PARTS + CROSS_PARTS
        reached = {tuple(k if axis == name else 0 for name in "xyz") for *_, axis in parts for k in (1, 2, 3)}
        for *_, axis in parts:
            for steps in rest(axis):
                reached.add(tuple(steps.get(name, 0) for name in "xyz"))
        reached = sorted((i, j, k) for i, j, k in reached if i > 0 or k % 2 == 1)
        return [self.sibling] + [self.step(*steps) for steps in reached]


def rest(axis):
    one, two = [name for name in "xyz" if name != axis]
    return [{one: i, two: j} for i in range(4) for j in range(4) if i or j]


def aligned(start, size):
    return pl.ds(pl.multiple_of(start, size), size)


class Reduction:
    def __init__(
        self, near, parts, full, partial, pair, first, first_in, second, second_in, send, recv
    ):
        self.near = near
        self.parts = parts
        self.partial, self.pair, self.full = partial, pair, full
        self.first, self.first_in = first, first_in
        self.second, self.second_in = second, second_in
        self.send, self.recv = send, recv
        self.half = pair.shape[0]
        self.size = self.half // 4
        self.base = near.core * self.half
        self.other = self.half - self.base
        self.slots = {}

    def copy(self, key, src, dst, device):
        slot = self.slots.setdefault(key, len(self.slots))
        return pltpu.make_async_remote_copy(
            src_ref=src,
            dst_ref=dst,
            send_sem=self.send.at[slot],
            recv_sem=self.recv.at[slot],
            device_id=device,
            device_id_type=MESH,
        )

    def arrived(self, key, place):
        self.copy(key, place, place, self.near.sibling).wait_recv()

    def left(self, key, place):
        self.copy(key, place, place, self.near.sibling).wait_send()

    def product(self, left, right):
        step = 256
        for side in (1, 0):
            start = self.base if side == 0 else self.other
            for i in range(self.half // step):
                rows = aligned(start + i * step, step)
                mixed = lax.dot_general(
                    left[:, rows],
                    right[...],
                    (((0,), (0,)), ((), ())),
                    preferred_element_type=jnp.float32,
                )
                self.partial[rows, :] = mixed.astype(jnp.bfloat16)
                if side == 1:
                    block = pl.ds(i * step, step)
                    self.copy(
                        ("pair", i), self.partial.at[rows], self.pair.at[block], self.near.sibling
                    ).start()

    def place(self, axis, k=0):
        return self.near.places[axis][k]

    def pair_sum(self):
        step = 256
        for i in range(self.half // step):
            block = pl.ds(i * step, step)
            self.arrived(("pair", i), self.pair.at[block])
            own = self.partial[aligned(self.base + i * step, step), :].astype(jnp.float32)
            total = own + self.pair[block, :].astype(jnp.float32)
            self.first[block, :] = total.astype(jnp.bfloat16)
        for k in (2, 1, 3):
            for part, (start, width, axis) in enumerate(self.parts):
                cols = pl.ds(start, width)
                self.copy(
                    ("first", part),
                    self.first.at[aligned(self.place(axis, k) * self.size, self.size), cols],
                    self.first_in.at[k - 1, :, cols],
                    self.near.step(**{axis: k}),
                ).start()

    def piece(self, part, steps, base=0):
        start, width, axis = self.parts[part]
        one, two = [name for name in "xyz" if name != axis]
        first, second = self.place(one, steps.get(one, 0)), self.place(two, steps.get(two, 0))
        row = (first * 2 + (second >> 1)) * 16 + base
        col = (second & 1) * (width // 2) + start
        return (aligned(row, 16), pl.ds(pl.multiple_of(col, LANES), width // 2))

    def landing(self, part):
        start, width, _ = self.parts[part]
        return pl.ds(start // 2, width // 2)

    def scatter_first(self):
        for part, (start, width, axis) in enumerate(self.parts):
            cols = pl.ds(start, width)
            self.arrived(("first", part), self.first_in.at[:, :, cols])
            total = self.first[aligned(self.place(axis) * self.size, self.size), cols].astype(jnp.float32)
            for k in range(3):
                total += self.first_in[k, :, cols].astype(jnp.float32)
            self.second[:, cols] = total.astype(jnp.bfloat16)
            for k, steps in enumerate(rest(axis)):
                self.copy(
                    ("second", part),
                    self.second.at[self.piece(part, steps)],
                    self.second_in.at[k, :, self.landing(part)],
                    self.near.step(**steps),
                ).start()

    def own_rows(self, part, k=0):
        return self.base + self.place(self.parts[part][2], k) * self.size

    def scatter_second(self):
        for part, (start, width, axis) in enumerate(self.parts):
            cols = self.landing(part)
            self.arrived(("second", part), self.second_in.at[:, :, cols])
            total = self.second[self.piece(part, {})].astype(jnp.float32)
            for k in range(15):
                total += self.second_in[k, :, cols].astype(jnp.float32)
            slices = self.piece(part, {}, self.own_rows(part))
            self.full[slices] = total.astype(jnp.bfloat16)
            place = self.full.at[slices]
            for steps in rest(axis):
                self.copy(("back", part), place, place, self.near.step(**steps)).start()

    def gather_second(self):
        for part, (start, width, axis) in enumerate(self.parts):
            cols = pl.ds(start, width)
            self.arrived(("back", part), self.second_in.at[:, :, self.landing(part)])
            place = self.full.at[aligned(self.own_rows(part), self.size), cols]
            for k in (2, 1, 3):
                self.copy(("last", part, 4 - k), place, place, self.near.step(**{axis: k})).start()
            self.copy(("across", part, 0), place, place, self.near.sibling).start()

    def gather_first(self):
        for k in (1, 3, 2):
            for part, (start, width, axis) in enumerate(self.parts):
                place = self.full.at[aligned(self.own_rows(part, k), self.size), pl.ds(start, width)]
                self.arrived(("last", part, k), place)
                self.copy(("across", part, k), place, place, self.near.sibling).start()

    def early_left(self):
        for i in range(self.half // 256):
            self.left(("pair", i), self.pair.at[pl.ds(i * 256, 256)])
        for part, (start, width, axis) in enumerate(self.parts):
            self.left(("first", part), self.first_in.at[:, :, pl.ds(start, width)])
            self.left(("second", part), self.second_in.at[:, :, self.landing(part)])

    def finish(self):
        turn = self.other - self.base
        for part, (start, width, axis) in enumerate(self.parts):
            cols = pl.ds(start, width)
            self.left(("back", part), self.second_in.at[:, :, self.landing(part)])
            block = self.full.at[pl.ds(0, self.size), cols]
            for k in (1, 2, 3):
                self.left(("last", part, k), block)
            for k in range(4):
                rows = aligned(self.own_rows(part, k) + turn, self.size)
                self.arrived(("across", part, k), self.full.at[rows, cols])
                self.left(("across", part, k), block)


def reduction_scratch(parts, width):
    half = width // 2
    kind = jnp.bfloat16
    slots = 2 + 10 * len(parts)
    return [
        pltpu.VMEM((width, width), kind),
        pltpu.VMEM((half, width), kind),
        pltpu.VMEM((half, width), kind),
        pltpu.VMEM((3, half // 4, width), kind),
        pltpu.VMEM((half // 4, width), kind),
        pltpu.VMEM((15, half // 32, width // 2), kind),
        pltpu.SemaphoreType.DMA((slots,)),
        pltpu.SemaphoreType.DMA((slots,)),
    ]


def layer_kernel(
    n,
    document,
    summary,
    encoder_gain,
    memory_gain,
    summary_gain,
    query_weight,
    key_weight,
    value_weight,
    output_weight,
    cross_query,
    cross_key,
    cross_value,
    cross_output,
    encoder_cotangent,
    decoder_cotangent,
    encoded,
    decoded,
    own_full,
    cross_full,
    doc,
    states,
    weights,
    own_cotangent,
    cross_cotangent,
    normed,
    qkv_send,
    qkv_recv,
    sq_send,
    sq_recv,
    head_send,
    head_recv,
    kv_send,
    kv_recv,
    early,
    cross_send,
    cross_recv,
    value_low,
    value_high,
    load_sem,
    send_sem,
    recv_sem,
    *grad_refs,
):
    dp = lax.axis_index("dp")
    me = lax.axis_index("ctx")
    rows = doc.shape[0]
    count = states.shape[0]
    width = doc.shape[1]
    blocks = width // (2 * LANES)

    loads = [
        pltpu.make_async_copy(src, dst, load_sem.at[i])
        for i, (src, dst) in enumerate(
            [
                (document, doc),
                (query_weight, weights.at[0]),
                (key_weight, weights.at[1]),
                (value_weight, weights.at[2]),
                (summary, states),
                (cross_query, weights.at[4]),
                (output_weight, weights.at[3]),
                (cross_key, weights.at[5]),
                (cross_value, weights.at[6]),
                (encoder_cotangent, own_cotangent),
                (cross_output, weights.at[7]),
                (decoder_cotangent, cross_cotangent),
            ]
        )
    ]
    for i in (0, 2, 3):
        loads[i].start()

    near = Neighbours(dp, me)
    barrier = pltpu.get_barrier_semaphore()

    @pl.loop(1, n)
    def _(i):
        peer = lax.rem(me + i, n)
        pl.semaphore_signal(barrier, inc=1, device_id=(dp, peer), device_id_type=MESH)

    others = near.distant()
    for device in others:
        pl.semaphore_signal(barrier, inc=1, device_id=device, device_id_type=MESH)

    def remote(phase, peer, source, src, dst):
        return pltpu.make_async_remote_copy(
            src_ref=src,
            dst_ref=dst,
            send_sem=send_sem.at[phase, peer],
            recv_sem=recv_sem.at[phase, source],
            device_id=(dp, peer),
            device_id_type=MESH,
        )

    def local(phase, src, dst):
        return pltpu.make_async_copy(src, dst, recv_sem.at[phase, me])

    def start(phase, peer, src, dst):
        @pl.when(peer != me)
        def _():
            remote(phase, peer, me, src, dst).start()

        @pl.when(peer == me)
        def _():
            local(phase, src, dst).start()

    def wait_one(phase, source, src, dst):
        @pl.when(source != me)
        def _():
            remote(phase, source, source, src, dst).wait_recv()

        @pl.when(source == me)
        def _():
            local(phase, src, dst).wait()

    def wait_all(phase, src_of, dst_of):
        @pl.loop(0, n)
        def _(source):
            wait_one(phase, source, src_of(source), dst_of(source))

    def wait_sent(phase, src_of, dst_of):
        @pl.loop(0, n)
        def _(peer):
            @pl.when(peer != me)
            def _():
                remote(phase, peer, me, src_of(peer), dst_of(peer)).wait_send()

    def column(index):
        return pl.ds(pl.multiple_of(index * LANES, LANES), LANES)

    def wide(index):
        return pl.ds(pl.multiple_of(index * 2 * LANES, 2 * LANES), 2 * LANES)

    loads[0].wait()
    normed[...] = norm_rows(doc[...], encoder_gain[...])
    pl.semaphore_wait(barrier, n - 1 + len(others))
    loads[2].wait()
    loads[3].wait()
    for i in (1, 4, 5, 6, 7, 8, 9, 10, 11):
        loads[i].start()

    @pl.loop(0, blocks)
    def _(i):
        block = lax.rem(lax.div(me, 2) + (blocks - 1) - i, blocks)
        for t in (1, 2):
            part = matmul(normed[...], weights[t, :, wide(block)]).astype(jnp.bfloat16)
            qkv_send[2 * block, t] = part[:, :LANES]
            qkv_send[2 * block + 1, t] = part[:, LANES:]
        for half in range(2):
            peer = 2 * block + half
            start(SELF_KV, peer, qkv_send.at[peer, pl.ds(1, 2)], qkv_recv.at[pl.ds(1, 2), me])

    loads[1].wait()

    @pl.loop(0, blocks)
    def _(i):
        part = matmul(normed[...], weights[0, :, wide(i)]).astype(jnp.bfloat16)
        qkv_send[2 * i, 0] = part[:, :LANES]
        qkv_send[2 * i + 1, 0] = part[:, LANES:]

    loads[4].wait()
    loads[5].wait()
    normed[0:count, :] = norm_rows(states[...], summary_gain[...])

    @pl.loop(0, blocks)
    def _(i):
        part = matmul(normed[0:count, :], weights[4, :, wide(i)]).astype(jnp.bfloat16)
        sq_send[2 * i] = part[:, :LANES]
        sq_send[2 * i + 1] = part[:, LANES:]

    kv_sent = lambda p: qkv_send.at[p, pl.ds(1, 2)], lambda p: qkv_recv.at[pl.ds(1, 2), me]
    wait_sent(SELF_KV, *kv_sent)

    @pl.loop(0, n)
    def _(i):
        peer = lax.rem(me + n - i, n)
        start(SELF_Q, peer, qkv_send.at[peer, 0], qkv_recv.at[0, me])

    lane = lax.broadcasted_iota(jnp.int32, (1, LANES), 1)
    low = lane < HEAD_DIM
    zero = jnp.zeros((), jnp.bfloat16)
    one = jnp.ones((), jnp.bfloat16)

    def set_values(ref):
        values = ref[...].reshape(n * rows, LANES)
        value_low[...] = jnp.where(low, values, one)
        value_high[...] = jnp.where(low, one, values)

    def attend_part(query, keys, places):
        def head(part, values):
            scores = lax.dot_general(
                part, keys, (((1,), (1,)), ((), ())), preferred_element_type=jnp.float32
            )
            top = jnp.max(scores, axis=-1, keepdims=True)
            weight = jnp.exp(scores - top).astype(jnp.bfloat16)
            return matmul(weight, values[places, :]), top

        left, left_top = head(jnp.where(low, query, zero), value_low)
        right, right_top = head(jnp.where(low, zero, query), value_high)
        mixed = jnp.where(low, left, right)
        total = jnp.where(
            low, pltpu.roll(left, HEAD_DIM, 1), pltpu.roll(right, HEAD_DIM, 1)
        )
        return mixed, total, jnp.where(low, left_top, right_top)

    def attend(query, keys):
        mixed, total, _ = attend_part(query, keys, pl.ds(0, n * rows))
        return (mixed / total).astype(jnp.bfloat16)

    wait_all(
        SELF_KV, lambda s: qkv_send.at[s, pl.ds(1, 2)], lambda s: qkv_recv.at[pl.ds(1, 2), s]
    )
    set_values(qkv_recv.at[2])

    @pl.loop(0, n)
    def _(i):
        peer = lax.rem(me + i, n)
        wait_one(SELF_Q, peer, qkv_send.at[peer, 0], qkv_recv.at[0, peer])
        keys = qkv_recv[1].reshape(n * rows, LANES)
        head_send[peer] = attend(qkv_recv[0, peer], keys)
        start(HEAD, peer, head_send.at[peer], head_recv.at[:, column(me)])

        @pl.when(i == 2)
        def _():
            @pl.loop(0, n)
            def _(p):
                start(SQ, p, sq_send.at[p], sq_recv.at[me])

    loads[6].wait()
    wait_all(HEAD, lambda s: head_send.at[s], lambda s: head_recv.at[:, column(s)])

    own_refs = Reduction(near, OWN_PARTS, own_full, *grad_refs[:REFS])
    cross_refs = Reduction(near, CROSS_PARTS, cross_full, *grad_refs[REFS:])
    loads[7].wait()
    loads[8].wait()

    for side, phase in enumerate((KV, KV_LATE)):
        place = pl.ds(side * (rows // 2), rows // 2)

        @pl.loop(0, blocks)
        def _(i):
            mixed = matmul(head_recv[place, :], weights[3, :, wide(i)])
            total = doc[place, wide(i)].astype(jnp.float32) + mixed
            encoded[place, wide(i)] = total.astype(jnp.bfloat16)

        normed[place, :] = norm_rows(encoded[place, :], memory_gain[...])

        @pl.loop(0, blocks)
        def _(i):
            block = lax.rem(lax.div(me, 2) + (blocks - 1) - i, blocks)
            for t in range(2):
                part = matmul(normed[place, :], weights[5 + t, :, wide(block)]).astype(jnp.bfloat16)
                kv_send[2 * block, side, t] = part[:, :LANES]
                kv_send[2 * block + 1, side, t] = part[:, LANES:]
            for half in range(2):
                peer = 2 * block + half
                start(phase, peer, kv_send.at[peer, side], kv_recv.at[side, :, me])

    loads[9].wait()
    own_refs.product(head_recv, own_cotangent)
    own_refs.pair_sum()

    wait_all(SQ, lambda s: sq_send.at[s], lambda s: sq_recv.at[s])
    span = n * rows // 2

    def ready(side, phase):
        wait_all(phase, lambda s: kv_send.at[s, side], lambda s: kv_recv.at[side, :, s])
        values = kv_recv[side, 1].reshape(span, LANES)
        value_low[pl.ds(side * span, span), :] = jnp.where(low, values, one)
        value_high[pl.ds(side * span, span), :] = jnp.where(low, one, values)

    def cross_part(pair, side):
        query = sq_recv[pl.ds(2 * pair, 2)].reshape(2 * count, LANES)
        keys = kv_recv[side, 0].reshape(span, LANES)
        return attend_part(query, keys, pl.ds(side * span, span))

    ready(0, KV)

    @pl.loop(0, n // 2)
    def _(pair):
        for t, value in enumerate(cross_part(pair, 0)):
            early[t, pair] = value

    ready(1, KV_LATE)

    def cross_block(i):
        pair = lax.rem(lax.div(me, 2) + 1 + i, n // 2)
        mixed, total, top = cross_part(pair, 1)
        best = jnp.maximum(top, early[2, pair])
        fade, late = jnp.exp(early[2, pair] - best), jnp.exp(top - best)
        mixed = mixed * late + early[0, pair] * fade
        total = total * late + early[1, pair] * fade
        mixed = (mixed / total).astype(jnp.bfloat16)
        cross_send[2 * pair] = mixed[:count]
        cross_send[2 * pair + 1] = mixed[count:]
        for half in range(2):
            peer = 2 * pair + half
            start(CROSS, peer, cross_send.at[peer], cross_recv.at[:, column(me)])

    pl.loop(0, n // 2 - 1)(cross_block)
    own_refs.scatter_first()
    cross_block(n // 2 - 1)
    loads[11].wait()
    wait_all(CROSS, lambda s: cross_send.at[s], lambda s: cross_recv.at[:, column(s)])
    cross_refs.product(cross_recv, cross_cotangent)
    own_refs.scatter_second()
    cross_refs.pair_sum()
    loads[10].wait()

    @pl.loop(0, blocks)
    def _(i):
        mixed = matmul(cross_recv[...], weights[7, :, wide(i)])
        decoded[:, wide(i)] = (states[:, wide(i)].astype(jnp.float32) + mixed).astype(jnp.bfloat16)

    own_refs.gather_second()
    cross_refs.scatter_first()
    cross_refs.scatter_second()
    own_refs.gather_first()
    wait_sent(SELF_Q, lambda p: qkv_send.at[p, 0], lambda p: qkv_recv.at[0, me])
    wait_sent(SQ, lambda p: sq_send.at[p], lambda p: sq_recv.at[me])
    wait_sent(HEAD, lambda p: head_send.at[p], lambda p: head_recv.at[:, column(me)])
    for side, phase in enumerate((KV, KV_LATE)):
        wait_sent(phase, lambda p: kv_send.at[p, side], lambda p: kv_recv.at[side, :, me])
    wait_sent(CROSS, lambda p: cross_send.at[p], lambda p: cross_recv.at[:, column(me)])
    cross_refs.gather_second()
    own_refs.early_left()
    cross_refs.early_left()
    own_refs.finish()
    cross_refs.gather_first()
    cross_refs.finish()


def store_kernel(*refs):
    copies = [
        pltpu.make_async_copy(src, dst, refs[8].at[i])
        for i, (src, dst) in enumerate(zip(refs[:4], refs[4:8]))
    ]
    for copy in copies:
        copy.start()
    for copy in copies:
        copy.wait()


def solution(mesh):
    n = mesh.shape["ctx"]

    def body(
        document,
        summary,
        encoder_gain,
        query_weight,
        key_weight,
        value_weight,
        output_weight,
        memory_gain,
        summary_gain,
        cross_query,
        cross_key,
        cross_value,
        cross_output,
        encoder_cotangent,
        decoder_cotangent,
    ):
        rows, width = document.shape[1:]
        count = summary.shape[1]
        half = jnp.bfloat16
        hbm = pl.BlockSpec(memory_space=pl.ANY)
        vmem = pl.BlockSpec(memory_space=pltpu.VMEM)
        shapes = [(rows, width), (count, width), (width, width), (width, width)]
        results = pl.pallas_call(
            functools.partial(layer_kernel, n),
            out_shape=[pltpu.VMEM(shape, half) for shape in shapes],
            in_specs=[hbm] * 2 + [vmem] * 3 + [hbm] * 10,
            out_specs=[vmem] * 4,
            scratch_shapes=[
                pltpu.VMEM((rows, width), half),
                pltpu.VMEM((count, width), half),
                pltpu.VMEM((8, width, width), half),
                pltpu.VMEM((rows, width), half),
                pltpu.VMEM((count, width), half),
                pltpu.VMEM((rows, width), half),
                pltpu.VMEM((n, 3, rows, LANES), half),
                pltpu.VMEM((3, n, rows, LANES), half),
                pltpu.VMEM((n, count, LANES), half),
                pltpu.VMEM((n, count, LANES), half),
                pltpu.VMEM((n, rows, LANES), half),
                pltpu.VMEM((rows, width), half),
                pltpu.VMEM((n, 2, 2, rows // 2, LANES), half),
                pltpu.VMEM((2, 2, n, rows // 2, LANES), half),
                pltpu.VMEM((3, n // 2, 2 * count, LANES), jnp.float32),
                pltpu.VMEM((n, count, LANES), half),
                pltpu.VMEM((count, width), half),
                pltpu.VMEM((n * rows, LANES), half),
                pltpu.VMEM((n * rows, LANES), half),
                pltpu.SemaphoreType.DMA((12,)),
                pltpu.SemaphoreType.DMA((7, n)),
                pltpu.SemaphoreType.DMA((7, n)),
                *reduction_scratch(OWN_PARTS, width),
                *reduction_scratch(CROSS_PARTS, width),
            ],
            compiler_params=pltpu.CompilerParams(
                collective_id=0, has_side_effects=True, vmem_limit_bytes=50 * 2**20
            ),
        )(
            document[0],
            summary[0],
            encoder_gain[None],
            memory_gain[None],
            summary_gain[None],
            query_weight,
            key_weight,
            value_weight,
            output_weight,
            cross_query,
            cross_key,
            cross_value,
            cross_output,
            encoder_cotangent[0],
            decoder_cotangent[0],
        )
        encoded, decoded, own_grad, cross_grad = pl.pallas_call(
            store_kernel,
            out_shape=[jax.ShapeDtypeStruct(shape, half) for shape in shapes],
            in_specs=[vmem] * 4,
            out_specs=[hbm] * 4,
            scratch_shapes=[pltpu.SemaphoreType.DMA((4,))],
            compiler_params=pltpu.CompilerParams(vmem_limit_bytes=4 * 2**20),
        )(*[pltpu.with_memory_space_constraint(result, pltpu.VMEM) for result in results])
        return (
            encoded[None],
            decoded[None],
            own_grad,
            cross_grad,
        )

    rows_spec = P("dp", "ctx", None)
    return jax.shard_map(
        body,
        mesh=mesh,
        in_specs=(rows_spec, rows_spec) + (P(),) * 11 + (rows_spec, rows_spec),
        out_specs=(rows_spec, rows_spec, P(), P()),
        check_vma=False,
    )
```

```python
import functools

import jax
import jax.numpy as jnp
from jax import lax
from jax.experimental import pallas as pl
from jax.experimental.pallas import tpu as pltpu
from jax.sharding import PartitionSpec as P

HEADS = 16
HEAD_DIM = 64
LANES = 128
MESH = pl.DeviceIdType.MESH
SELF_KV, SELF_Q, SQ, HEAD, KV, KV_LATE, CROSS = range(7)


def norm_rows(rows, gain):
    values = rows.astype(jnp.float32)
    scale = lax.rsqrt(jnp.mean(values * values, axis=-1, keepdims=True) + 1e-06)
    return (values * scale * gain).astype(jnp.bfloat16)


def matmul(left, right):
    return jnp.dot(left, right, preferred_element_type=jnp.float32)


OWN_PARTS = ((0, 512, "x"), (512, 256, "y"), (768, 256, "z"))
CROSS_PARTS = ((0, 512, "y"), (512, 256, "z"), (768, 256, "x"))
REFS = 8


class Neighbours:
    def __init__(self, dp, ctx):
        self.core = dp & 1
        low, high = (dp >> 1) & 1, ctx >> 2
        place = {"x": dp >> 2, "y": ctx & 3, "z": high * 2 + low}
        self.places = {axis: [(start + k) & 3 for k in range(4)] for axis, start in place.items()}
        self.dp_x = [x * 4 for x in self.places["x"]]
        self.dp_z = [(z & 1) * 2 + self.core for z in self.places["z"]]
        self.ctx_z = [(z >> 1) * 4 for z in self.places["z"]]
        self.sibling = (dp + 1 - 2 * self.core, ctx)

    def step(self, x=0, y=0, z=0):
        return (self.dp_x[x] + self.dp_z[z], self.ctx_z[z] + self.places["y"][y])

    def distant(self):
        parts = OWN_PARTS + CROSS_PARTS
        reached = {tuple(k if axis == name else 0 for name in "xyz") for *_, axis in parts for k in (1, 2, 3)}
        for *_, axis in parts:
            for steps in rest(axis):
                reached.add(tuple(steps.get(name, 0) for name in "xyz"))
        reached = sorted((i, j, k) for i, j, k in reached if i > 0 or k % 2 == 1)
        return [self.sibling] + [self.step(*steps) for steps in reached]


def rest(axis):
    one, two = [name for name in "xyz" if name != axis]
    return [{one: i, two: j} for i in range(4) for j in range(4) if i or j]


def aligned(start, size):
    return pl.ds(pl.multiple_of(start, size), size)


class Reduction:
    def __init__(
        self, near, parts, full, partial, pair, first, first_in, second, second_in, send, recv
    ):
        self.near = near
        self.parts = parts
        self.partial, self.pair, self.full = partial, pair, full
        self.first, self.first_in = first, first_in
        self.second, self.second_in = second, second_in
        self.send, self.recv = send, recv
        self.half = pair.shape[0]
        self.size = self.half // 4
        self.base = near.core * self.half
        self.other = self.half - self.base
        self.slots = {}

    def copy(self, key, src, dst, device):
        slot = self.slots.setdefault(key, len(self.slots))
        return pltpu.make_async_remote_copy(
            src_ref=src,
            dst_ref=dst,
            send_sem=self.send.at[slot],
            recv_sem=self.recv.at[slot],
            device_id=device,
            device_id_type=MESH,
        )

    def arrived(self, key, place):
        self.copy(key, place, place, self.near.sibling).wait_recv()

    def left(self, key, place):
        self.copy(key, place, place, self.near.sibling).wait_send()

    def product(self, left, right):
        step = 256
        for side in (1, 0):
            start = self.base if side == 0 else self.other
            for i in range(self.half // step):
                rows = aligned(start + i * step, step)
                mixed = lax.dot_general(
                    left[:, rows],
                    right[...],
                    (((0,), (0,)), ((), ())),
                    preferred_element_type=jnp.float32,
                )
                self.partial[rows, :] = mixed.astype(jnp.bfloat16)
                if side == 1:
                    block = pl.ds(i * step, step)
                    self.copy(
                        ("pair", i), self.partial.at[rows], self.pair.at[block], self.near.sibling
                    ).start()

    def place(self, axis, k=0):
        return self.near.places[axis][k]

    def pair_sum(self):
        step = 256
        for i in range(self.half // step):
            block = pl.ds(i * step, step)
            self.arrived(("pair", i), self.pair.at[block])
            own = self.partial[aligned(self.base + i * step, step), :].astype(jnp.float32)
            total = own + self.pair[block, :].astype(jnp.float32)
            self.first[block, :] = total.astype(jnp.bfloat16)
        for k in (2, 1, 3):
            for part, (start, width, axis) in enumerate(self.parts):
                cols = pl.ds(start, width)
                self.copy(
                    ("first", part),
                    self.first.at[aligned(self.place(axis, k) * self.size, self.size), cols],
                    self.first_in.at[k - 1, :, cols],
                    self.near.step(**{axis: k}),
                ).start()

    def piece(self, part, steps, base=0):
        start, width, axis = self.parts[part]
        one, two = [name for name in "xyz" if name != axis]
        first, second = self.place(one, steps.get(one, 0)), self.place(two, steps.get(two, 0))
        row = (first * 2 + (second >> 1)) * 16 + base
        col = (second & 1) * (width // 2) + start
        return (aligned(row, 16), pl.ds(pl.multiple_of(col, LANES), width // 2))

    def landing(self, part):
        start, width, _ = self.parts[part]
        return pl.ds(start // 2, width // 2)

    def scatter_first(self):
        for part, (start, width, axis) in enumerate(self.parts):
            cols = pl.ds(start, width)
            self.arrived(("first", part), self.first_in.at[:, :, cols])
            total = self.first[aligned(self.place(axis) * self.size, self.size), cols].astype(jnp.float32)
            for k in range(3):
                total += self.first_in[k, :, cols].astype(jnp.float32)
            self.second[:, cols] = total.astype(jnp.bfloat16)
            for k, steps in enumerate(rest(axis)):
                self.copy(
                    ("second", part),
                    self.second.at[self.piece(part, steps)],
                    self.second_in.at[k, :, self.landing(part)],
                    self.near.step(**steps),
                ).start()

    def own_rows(self, part, k=0):
        return self.base + self.place(self.parts[part][2], k) * self.size

    def scatter_second(self):
        for part, (start, width, axis) in enumerate(self.parts):
            cols = self.landing(part)
            self.arrived(("second", part), self.second_in.at[:, :, cols])
            total = self.second[self.piece(part, {})].astype(jnp.float32)
            for k in range(15):
                total += self.second_in[k, :, cols].astype(jnp.float32)
            slices = self.piece(part, {}, self.own_rows(part))
            self.full[slices] = total.astype(jnp.bfloat16)
            place = self.full.at[slices]
            for steps in rest(axis):
                self.copy(("back", part), place, place, self.near.step(**steps)).start()

    def gather_second(self):
        for part, (start, width, axis) in enumerate(self.parts):
            cols = pl.ds(start, width)
            self.arrived(("back", part), self.second_in.at[:, :, self.landing(part)])
            place = self.full.at[aligned(self.own_rows(part), self.size), cols]
            for k in (2, 1, 3):
                self.copy(("last", part, 4 - k), place, place, self.near.step(**{axis: k})).start()
            self.copy(("across", part, 0), place, place, self.near.sibling).start()

    def gather_first(self):
        for k in (1, 3, 2):
            for part, (start, width, axis) in enumerate(self.parts):
                place = self.full.at[aligned(self.own_rows(part, k), self.size), pl.ds(start, width)]
                self.arrived(("last", part, k), place)
                self.copy(("across", part, k), place, place, self.near.sibling).start()

    def early_left(self):
        for i in range(self.half // 256):
            self.left(("pair", i), self.pair.at[pl.ds(i * 256, 256)])
        for part, (start, width, axis) in enumerate(self.parts):
            self.left(("first", part), self.first_in.at[:, :, pl.ds(start, width)])
            self.left(("second", part), self.second_in.at[:, :, self.landing(part)])

    def finish(self):
        turn = self.other - self.base
        for part, (start, width, axis) in enumerate(self.parts):
            cols = pl.ds(start, width)
            self.left(("back", part), self.second_in.at[:, :, self.landing(part)])
            block = self.full.at[pl.ds(0, self.size), cols]
            for k in (1, 2, 3):
                self.left(("last", part, k), block)
            for k in range(4):
                rows = aligned(self.own_rows(part, k) + turn, self.size)
                self.arrived(("across", part, k), self.full.at[rows, cols])
                self.left(("across", part, k), block)


def reduction_scratch(parts, width):
    half = width // 2
    kind = jnp.bfloat16
    slots = 2 + 10 * len(parts)
    return [
        pltpu.VMEM((width, width), kind),
        pltpu.VMEM((half, width), kind),
        pltpu.VMEM((half, width), kind),
        pltpu.VMEM((3, half // 4, width), kind),
        pltpu.VMEM((half // 4, width), kind),
        pltpu.VMEM((15, half // 32, width // 2), kind),
        pltpu.SemaphoreType.DMA((slots,)),
        pltpu.SemaphoreType.DMA((slots,)),
    ]


def layer_kernel(
    n,
    document,
    summary,
    encoder_gain,
    memory_gain,
    summary_gain,
    query_weight,
    key_weight,
    value_weight,
    output_weight,
    cross_query,
    cross_key,
    cross_value,
    cross_output,
    encoder_cotangent,
    decoder_cotangent,
    encoded,
    decoded,
    own_full,
    cross_full,
    doc,
    states,
    weights,
    own_cotangent,
    cross_cotangent,
    normed,
    qkv_send,
    qkv_recv,
    sq_send,
    sq_recv,
    head_send,
    head_recv,
    kv_send,
    kv_recv,
    early,
    cross_send,
    cross_recv,
    value_low,
    value_high,
    load_sem,
    send_sem,
    recv_sem,
    *grad_refs,
):
    dp = lax.axis_index("dp")
    me = lax.axis_index("ctx")
    rows = doc.shape[0]
    count = states.shape[0]
    width = doc.shape[1]
    blocks = width // (2 * LANES)

    loads = [
        pltpu.make_async_copy(src, dst, load_sem.at[i])
        for i, (src, dst) in enumerate(
            [
                (document, doc),
                (query_weight, weights.at[0]),
                (key_weight, weights.at[1]),
                (value_weight, weights.at[2]),
                (summary, states),
                (cross_query, weights.at[4]),
                (output_weight, weights.at[3]),
                (cross_key, weights.at[5]),
                (cross_value, weights.at[6]),
                (encoder_cotangent, own_cotangent),
                (cross_output, weights.at[7]),
                (decoder_cotangent, cross_cotangent),
            ]
        )
    ]
    for i in (0, 2, 3):
        loads[i].start()

    near = Neighbours(dp, me)
    barrier = pltpu.get_barrier_semaphore()

    @pl.loop(1, n)
    def _(i):
        peer = lax.rem(me + i, n)
        pl.semaphore_signal(barrier, inc=1, device_id=(dp, peer), device_id_type=MESH)

    others = near.distant()
    for device in others:
        pl.semaphore_signal(barrier, inc=1, device_id=device, device_id_type=MESH)

    def remote(phase, peer, source, src, dst):
        return pltpu.make_async_remote_copy(
            src_ref=src,
            dst_ref=dst,
            send_sem=send_sem.at[phase, peer],
            recv_sem=recv_sem.at[phase, source],
            device_id=(dp, peer),
            device_id_type=MESH,
        )

    def local(phase, src, dst):
        return pltpu.make_async_copy(src, dst, recv_sem.at[phase, me])

    def start(phase, peer, src, dst):
        @pl.when(peer != me)
        def _():
            remote(phase, peer, me, src, dst).start()

        @pl.when(peer == me)
        def _():
            local(phase, src, dst).start()

    def wait_one(phase, source, src, dst):
        @pl.when(source != me)
        def _():
            remote(phase, source, source, src, dst).wait_recv()

        @pl.when(source == me)
        def _():
            local(phase, src, dst).wait()

    def wait_all(phase, src_of, dst_of):
        @pl.loop(0, n)
        def _(source):
            wait_one(phase, source, src_of(source), dst_of(source))

    def wait_sent(phase, src_of, dst_of):
        @pl.loop(0, n)
        def _(peer):
            @pl.when(peer != me)
            def _():
                remote(phase, peer, me, src_of(peer), dst_of(peer)).wait_send()

    def column(index):
        return pl.ds(pl.multiple_of(index * LANES, LANES), LANES)

    def wide(index):
        return pl.ds(pl.multiple_of(index * 2 * LANES, 2 * LANES), 2 * LANES)

    loads[0].wait()
    normed[...] = norm_rows(doc[...], encoder_gain[...])
    pl.semaphore_wait(barrier, n - 1 + len(others))
    loads[2].wait()
    loads[3].wait()
    for i in (1, 4, 5, 6, 7, 8, 9, 10, 11):
        loads[i].start()

    @pl.loop(0, blocks)
    def _(i):
        block = lax.rem(lax.div(me, 2) + (blocks - 1) - i, blocks)
        for t in (1, 2):
            part = matmul(normed[...], weights[t, :, wide(block)]).astype(jnp.bfloat16)
            qkv_send[2 * block, t] = part[:, :LANES]
            qkv_send[2 * block + 1, t] = part[:, LANES:]
        for half in range(2):
            peer = 2 * block + half
            start(SELF_KV, peer, qkv_send.at[peer, pl.ds(1, 2)], qkv_recv.at[pl.ds(1, 2), me])

    loads[1].wait()

    @pl.loop(0, blocks)
    def _(i):
        part = matmul(normed[...], weights[0, :, wide(i)]).astype(jnp.bfloat16)
        qkv_send[2 * i, 0] = part[:, :LANES]
        qkv_send[2 * i + 1, 0] = part[:, LANES:]

    loads[4].wait()
    loads[5].wait()
    normed[0:count, :] = norm_rows(states[...], summary_gain[...])

    @pl.loop(0, blocks)
    def _(i):
        part = matmul(normed[0:count, :], weights[4, :, wide(i)]).astype(jnp.bfloat16)
        sq_send[2 * i] = part[:, :LANES]
        sq_send[2 * i + 1] = part[:, LANES:]

    kv_sent = lambda p: qkv_send.at[p, pl.ds(1, 2)], lambda p: qkv_recv.at[pl.ds(1, 2), me]
    wait_sent(SELF_KV, *kv_sent)

    @pl.loop(0, n)
    def _(i):
        peer = lax.rem(me + n - i, n)
        start(SELF_Q, peer, qkv_send.at[peer, 0], qkv_recv.at[0, me])

    lane = lax.broadcasted_iota(jnp.int32, (1, LANES), 1)
    low = lane < HEAD_DIM
    zero = jnp.zeros((), jnp.bfloat16)
    one = jnp.ones((), jnp.bfloat16)

    def set_values(ref):
        values = ref[...].reshape(n * rows, LANES)
        value_low[...] = jnp.where(low, values, one)
        value_high[...] = jnp.where(low, one, values)

    def attend_part(query, keys, places):
        def head(part, values):
            scores = lax.dot_general(
                part, keys, (((1,), (1,)), ((), ())), preferred_element_type=jnp.float32
            )
            top = jnp.max(scores, axis=-1, keepdims=True)
            weight = jnp.exp(scores - top).astype(jnp.bfloat16)
            return matmul(weight, values[places, :]), top

        left, left_top = head(jnp.where(low, query, zero), value_low)
        right, right_top = head(jnp.where(low, zero, query), value_high)
        mixed = jnp.where(low, left, right)
        total = jnp.where(
            low, pltpu.roll(left, HEAD_DIM, 1), pltpu.roll(right, HEAD_DIM, 1)
        )
        return mixed, total, jnp.where(low, left_top, right_top)

    def attend(query, keys):
        mixed, total, _ = attend_part(query, keys, pl.ds(0, n * rows))
        return (mixed / total).astype(jnp.bfloat16)

    wait_all(
        SELF_KV, lambda s: qkv_send.at[s, pl.ds(1, 2)], lambda s: qkv_recv.at[pl.ds(1, 2), s]
    )
    set_values(qkv_recv.at[2])

    @pl.loop(0, n)
    def _(i):
        peer = lax.rem(me + i, n)
        wait_one(SELF_Q, peer, qkv_send.at[peer, 0], qkv_recv.at[0, peer])
        keys = qkv_recv[1].reshape(n * rows, LANES)
        head_send[peer] = attend(qkv_recv[0, peer], keys)
        start(HEAD, peer, head_send.at[peer], head_recv.at[:, column(me)])

        @pl.when(i == 2)
        def _():
            @pl.loop(0, n)
            def _(p):
                start(SQ, p, sq_send.at[p], sq_recv.at[me])

    loads[6].wait()
    wait_all(HEAD, lambda s: head_send.at[s], lambda s: head_recv.at[:, column(s)])

    own_refs = Reduction(near, OWN_PARTS, own_full, *grad_refs[:REFS])
    cross_refs = Reduction(near, CROSS_PARTS, cross_full, *grad_refs[REFS:])
    loads[7].wait()
    loads[8].wait()

    for side, phase in enumerate((KV, KV_LATE)):
        place = pl.ds(side * (rows // 2), rows // 2)

        @pl.loop(0, blocks)
        def _(i):
            mixed = matmul(head_recv[place, :], weights[3, :, wide(i)])
            total = doc[place, wide(i)].astype(jnp.float32) + mixed
            encoded[place, wide(i)] = total.astype(jnp.bfloat16)

        normed[place, :] = norm_rows(encoded[place, :], memory_gain[...])

        @pl.loop(0, blocks)
        def _(i):
            block = lax.rem(lax.div(me, 2) + (blocks - 1) - i, blocks)
            for t in range(2):
                part = matmul(normed[place, :], weights[5 + t, :, wide(block)]).astype(jnp.bfloat16)
                kv_send[2 * block, side, t] = part[:, :LANES]
                kv_send[2 * block + 1, side, t] = part[:, LANES:]
            for half in range(2):
                peer = 2 * block + half
                start(phase, peer, kv_send.at[peer, side], kv_recv.at[side, :, me])

    loads[9].wait()
    own_refs.product(head_recv, own_cotangent)
    own_refs.pair_sum()

    wait_all(SQ, lambda s: sq_send.at[s], lambda s: sq_recv.at[s])
    span = n * rows // 2

    def ready(side, phase):
        wait_all(phase, lambda s: kv_send.at[s, side], lambda s: kv_recv.at[side, :, s])
        values = kv_recv[side, 1].reshape(span, LANES)
        value_low[pl.ds(side * span, span), :] = jnp.where(low, values, one)
        value_high[pl.ds(side * span, span), :] = jnp.where(low, one, values)

    def cross_part(pair, side):
        query = sq_recv[pl.ds(2 * pair, 2)].reshape(2 * count, LANES)
        keys = kv_recv[side, 0].reshape(span, LANES)
        return attend_part(query, keys, pl.ds(side * span, span))

    ready(0, KV)

    @pl.loop(0, n // 2)
    def _(pair):
        for t, value in enumerate(cross_part(pair, 0)):
            early[t, pair] = value

    ready(1, KV_LATE)

    def cross_block(i):
        pair = lax.rem(lax.div(me, 2) + 1 + i, n // 2)
        mixed, total, top = cross_part(pair, 1)
        best = jnp.maximum(top, early[2, pair])
        fade, late = jnp.exp(early[2, pair] - best), jnp.exp(top - best)
        mixed = mixed * late + early[0, pair] * fade
        total = total * late + early[1, pair] * fade
        mixed = (mixed / total).astype(jnp.bfloat16)
        cross_send[2 * pair] = mixed[:count]
        cross_send[2 * pair + 1] = mixed[count:]
        for half in range(2):
            peer = 2 * pair + half
            start(CROSS, peer, cross_send.at[peer], cross_recv.at[:, column(me)])

    pl.loop(0, n // 2 - 1)(cross_block)
    own_refs.scatter_first()
    cross_block(n // 2 - 1)
    loads[11].wait()
    wait_all(CROSS, lambda s: cross_send.at[s], lambda s: cross_recv.at[:, column(s)])
    cross_refs.product(cross_recv, cross_cotangent)
    own_refs.scatter_second()
    cross_refs.pair_sum()
    loads[10].wait()

    @pl.loop(0, blocks)
    def _(i):
        mixed = matmul(cross_recv[...], weights[7, :, wide(i)])
        decoded[:, wide(i)] = (states[:, wide(i)].astype(jnp.float32) + mixed).astype(jnp.bfloat16)

    own_refs.gather_second()
    cross_refs.scatter_first()
    cross_refs.scatter_second()
    wait_sent(SELF_Q, lambda p: qkv_send.at[p, 0], lambda p: qkv_recv.at[0, me])
    wait_sent(SQ, lambda p: sq_send.at[p], lambda p: sq_recv.at[me])
    wait_sent(HEAD, lambda p: head_send.at[p], lambda p: head_recv.at[:, column(me)])
    for side, phase in enumerate((KV, KV_LATE)):
        wait_sent(phase, lambda p: kv_send.at[p, side], lambda p: kv_recv.at[side, :, me])
    wait_sent(CROSS, lambda p: cross_send.at[p], lambda p: cross_recv.at[:, column(me)])
    cross_refs.gather_second()
    own_refs.gather_first()
    own_refs.early_left()
    cross_refs.early_left()
    own_refs.finish()
    cross_refs.gather_first()
    cross_refs.finish()


def store_kernel(*refs):
    copies = [
        pltpu.make_async_copy(src, dst, refs[8].at[i])
        for i, (src, dst) in enumerate(zip(refs[:4], refs[4:8]))
    ]
    for copy in copies:
        copy.start()
    for copy in copies:
        copy.wait()


def solution(mesh):
    n = mesh.shape["ctx"]

    def body(
        document,
        summary,
        encoder_gain,
        query_weight,
        key_weight,
        value_weight,
        output_weight,
        memory_gain,
        summary_gain,
        cross_query,
        cross_key,
        cross_value,
        cross_output,
        encoder_cotangent,
        decoder_cotangent,
    ):
        rows, width = document.shape[1:]
        count = summary.shape[1]
        half = jnp.bfloat16
        hbm = pl.BlockSpec(memory_space=pl.ANY)
        vmem = pl.BlockSpec(memory_space=pltpu.VMEM)
        shapes = [(rows, width), (count, width), (width, width), (width, width)]
        results = pl.pallas_call(
            functools.partial(layer_kernel, n),
            out_shape=[pltpu.VMEM(shape, half) for shape in shapes],
            in_specs=[hbm] * 2 + [vmem] * 3 + [hbm] * 10,
            out_specs=[vmem] * 4,
            scratch_shapes=[
                pltpu.VMEM((rows, width), half),
                pltpu.VMEM((count, width), half),
                pltpu.VMEM((8, width, width), half),
                pltpu.VMEM((rows, width), half),
                pltpu.VMEM((count, width), half),
                pltpu.VMEM((rows, width), half),
                pltpu.VMEM((n, 3, rows, LANES), half),
                pltpu.VMEM((3, n, rows, LANES), half),
                pltpu.VMEM((n, count, LANES), half),
                pltpu.VMEM((n, count, LANES), half),
                pltpu.VMEM((n, rows, LANES), half),
                pltpu.VMEM((rows, width), half),
                pltpu.VMEM((n, 2, 2, rows // 2, LANES), half),
                pltpu.VMEM((2, 2, n, rows // 2, LANES), half),
                pltpu.VMEM((3, n // 2, 2 * count, LANES), jnp.float32),
                pltpu.VMEM((n, count, LANES), half),
                pltpu.VMEM((count, width), half),
                pltpu.VMEM((n * rows, LANES), half),
                pltpu.VMEM((n * rows, LANES), half),
                pltpu.SemaphoreType.DMA((12,)),
                pltpu.SemaphoreType.DMA((7, n)),
                pltpu.SemaphoreType.DMA((7, n)),
                *reduction_scratch(OWN_PARTS, width),
                *reduction_scratch(CROSS_PARTS, width),
            ],
            compiler_params=pltpu.CompilerParams(
                collective_id=0, has_side_effects=True, vmem_limit_bytes=50 * 2**20
            ),
        )(
            document[0],
            summary[0],
            encoder_gain[None],
            memory_gain[None],
            summary_gain[None],
            query_weight,
            key_weight,
            value_weight,
            output_weight,
            cross_query,
            cross_key,
            cross_value,
            cross_output,
            encoder_cotangent[0],
            decoder_cotangent[0],
        )
        encoded, decoded, own_grad, cross_grad = pl.pallas_call(
            store_kernel,
            out_shape=[jax.ShapeDtypeStruct(shape, half) for shape in shapes],
            in_specs=[vmem] * 4,
            out_specs=[hbm] * 4,
            scratch_shapes=[pltpu.SemaphoreType.DMA((4,))],
            compiler_params=pltpu.CompilerParams(vmem_limit_bytes=4 * 2**20),
        )(*[pltpu.with_memory_space_constraint(result, pltpu.VMEM) for result in results])
        return (
            encoded[None],
            decoded[None],
            own_grad,
            cross_grad,
        )

    rows_spec = P("dp", "ctx", None)
    return jax.shard_map(
        body,
        mesh=mesh,
        in_specs=(rows_spec, rows_spec) + (P(),) * 11 + (rows_spec, rows_spec),
        out_specs=(rows_spec, rows_spec, P(), P()),
        check_vma=False,
    )
```
